256 devices in a mesh: pipe: 8 (over y, x_lo), dp: 32 (over x_hi, z, core).
Axes of the slice: x: 4 (x_hi: 2, x_lo: 2; x = x_hi * 2 + x_lo), y: 4, z: 8, core: 2. Of those that a mesh axis runs over, the one named last changes fastest.
Arguments:
- acts: bfloat16 [8, 8192, 3072], P('pipe', 'dp'), may hold values from -24 to 24, as said below
- grad: float32 [24576, 4096], P('pipe', 'dp'), may hold values from -6 to 6
- owner_of: int32 [8, 12], replicated, may hold values from 0 to 7, as said below
Outputs:
- precond: float32 [24576, 4096], P('pipe', 'dp')
- held_inverse: float32 [8, 24, 256, 256], P('pipe', None, 'dp')
The draws below stay inside these ranges and needn't reach their ends.
Inputs may be any that keep to these rules, and one draw needn't show every extreme that they name: `acts`: column and token scales of the activations vary; entries lie within the range. `owner_of`: no section index owns more than 24 blocks in all, and some section index owns exactly 24.
All inputs are finite; a program needn't handle non-finite values.
Results may differ from the reference program's by a relative error of at most 0.0003.
Values sent between devices are 32-bit elements; how exact they have to be, the bound alone decides.
No kernel may reach another device: no remote copies, remote signals or barrier semaphores. Data moves between devices by JAX's collectives and lax.ppermute only.
A program may use at most 64 MiB of HBM per device.

```python
import math
import jax
import jax.numpy as jnp
from jax import lax

W = 3072
GO = 4096
BLK = 256
NB = 12
HOST = 24
TOKENS = 8192
N_PIPE = 8


def draw_acts(key, part):
    keys = jax.random.split(key, 3)
    shape = (N_PIPE, TOKENS, W)
    col_scale = jnp.exp(jax.random.uniform(keys[1], (N_PIPE, 1, W), jnp.float32, math.log(0.3), math.log(3.0)))
    row_scale = jnp.exp(jax.random.uniform(keys[2], (N_PIPE, TOKENS, 1), jnp.float32, math.log(0.5), math.log(2.0)))
    base = jax.random.normal(keys[0], shape, jnp.float32)
    base = jnp.clip(base, -4.0, 4.0)
    return (base * col_scale * row_scale).astype(jnp.bfloat16)


def draw_owner_of(key, part):
    keys = jax.random.split(jax.random.fold_in(key, 17), 3)
    slot_total = N_PIPE * HOST
    busiest = jax.random.randint(keys[0], (), 0, N_PIPE)
    scores = jax.random.permutation(keys[1], slot_total).astype(jnp.int32)
    slot_ids = jnp.arange(slot_total, dtype=jnp.int32)
    scores = jnp.where(slot_ids // HOST == busiest, scores - slot_total, scores)
    ordered = jnp.argsort(scores, stable=True).astype(jnp.int32)
    chosen = ordered[:N_PIPE * NB] // HOST
    mixing = jax.random.permutation(keys[2], N_PIPE * NB)
    return chosen[mixing].reshape(N_PIPE, NB).astype(jnp.int32)


def block_scale(rng, extent, shards, least, high):
    def one(axis_at, blocks):
        draws = jax.random.uniform(jax.random.fold_in(jax.random.fold_in(rng, 6), axis_at), (blocks,), jnp.float32, least / len(shards), high / len(shards))
        return jnp.repeat(jnp.exp(draws), extent[axis_at] // blocks).reshape((-1,) + (1,) * (len(extent) - axis_at - 1))

    level = one(*shards[0])
    for cut in shards[1:]:
        level = level * one(*cut)
    return level


def noise(stream_key, dims, scale, limit, cuts=(), held_as=jnp.bfloat16):
    result = scale * jax.random.normal(stream_key, dims, jnp.float32)
    if cuts:
        result = result * block_scale(stream_key, dims, cuts, -0.22, 0.18)
    return jnp.clip(result, -limit, limit).astype(held_as)


def setup_inputs(seed: int = 0) -> dict:
    arg_keys = jax.random.split(jax.random.key(seed), 4)
    return {
        "acts": draw_acts(jax.random.fold_in(arg_keys[3], 71), 0),
        "grad": noise(arg_keys[1], (N_PIPE * W, GO), 1.0, 6.0, ((0, 8), (1, 32)), jnp.float32),
        "owner_of": draw_owner_of(jax.random.fold_in(arg_keys[3], 71), 0),
    }


damping_ratio = 0.1

def invert_blocks(factor, vacant):
    order_size = factor.shape[-1]
    diagonal_sum = jnp.sum(jnp.diagonal(factor, axis1=1, axis2=2), axis=1)
    damping = damping_ratio * diagonal_sum / order_size
    identity = jnp.eye(order_size, dtype=factor.dtype)
    shifted = factor + (damping + vacant)[:, None, None] * identity
    cholesky_lower = jnp.linalg.cholesky(shifted)
    identity_stack = jnp.broadcast_to(identity, factor.shape)
    inv_lower = lax.linalg.triangular_solve(cholesky_lower, identity_stack, left_side=True, lower=True)
    return jnp.einsum('mkr,mkc->mrc', inv_lower, inv_lower, precision=lax.Precision.HIGHEST)

def slot_tables(owner_of):
    owners_flat = owner_of.reshape(-1).astype(jnp.int32)
    positions = jnp.arange(owners_flat.shape[0], dtype=jnp.int32)
    matches = owners_flat[:, None] == owners_flat[None, :]
    before = positions[None, :] < positions[:, None]
    slot_rank = jnp.sum((matches & before).astype(jnp.int32), axis=1)
    return (owners_flat, slot_rank)

def reference(acts, grad, owner_of):

    def per_section(section_acts):
        blocks = []
        for block_id in range(NB):
            columns = section_acts[:, block_id * BLK:(block_id + 1) * BLK]
            blocks.append(jnp.dot(columns.T.astype(jnp.float32), columns.astype(jnp.float32), preferred_element_type=jnp.float32))
        factor = jnp.stack(blocks) / TOKENS
        return invert_blocks(factor, jnp.zeros((NB,), factor.dtype))
    inverse = lax.map(per_section, acts)
    precond = jnp.einsum('sbrk,sbkc->sbrc', inverse, grad.reshape(N_PIPE, NB, BLK, GO), precision=lax.Precision.HIGHEST)
    precond = precond.reshape(N_PIPE * W, GO)
    owners_flat, slot_rank = slot_tables(owner_of)
    pipe_ids = jnp.arange(N_PIPE, dtype=jnp.int32)
    slot_ids = jnp.arange(HOST, dtype=jnp.int32)
    selector = (owners_flat[None, None, :] == pipe_ids[:, None, None]) & (slot_rank[None, None, :] == slot_ids[None, :, None])
    selector = selector.astype(inverse.dtype)
    held_inverse = jnp.einsum('pjk,krc->pjrc', selector, inverse.reshape(N_PIPE * NB, BLK, BLK), precision=lax.Precision.HIGHEST)
    return (precond, held_inverse)
```

```python
import functools

import jax
import jax.numpy as jnp
from jax import lax
from jax.experimental import pallas as pl
from jax.experimental.pallas import tpu as pltpu
from jax.sharding import Mesh
from jax.sharding import PartitionSpec as P

BLK = 256
HALF = BLK // 2
SUB = 8
NB = 12
PER_CORE = NB // 2
HOST = 24
TALL = HALF + SUB
N_Z = 8
DP = ("x", "z", "c")
damping_ratio = 0.1
VMEM = pltpu.VMEM
f32 = jnp.float32


def holds(z, c):
    return (z % 4) != jnp.where(c == 0, 3, 1)


def rank(z, c):
    return (z // 4) * 3 + jnp.where(c == 0, z % 4, (z % 4 + 1) // 2)


def held_by(z, c):
    return z % 4 != (3 if c == 0 else 1)


def place_of(zc_step):
    into = [
        (z * 2 + c, (z + zc_step) % N_Z * 2 + c)
        for z in range(N_Z)
        for c in range(2)
        if held_by((z + zc_step) % N_Z, c)
    ]
    out = [
        (z * 2 + c, (z + zc_step) % N_Z * 2 + c)
        for z in range(N_Z)
        for c in range(2)
        if held_by(z, c)
    ]
    return into, out


def grids():
    return (
        lax.broadcasted_iota(jnp.int32, (HALF, HALF), 0),
        lax.broadcasted_iota(jnp.int32, (HALF, HALF), 1),
    )


def store_packed(ref, upper, cross, lower):
    i, j = grids()
    ref[0:HALF, 0:HALF] = cross
    ref[0:HALF, HALF:BLK] = jnp.where(i >= j, upper, lower)
    ref[HALF:TALL, 0:HALF] = jnp.broadcast_to(
        jnp.sum(jnp.where(i == j, lower, 0.0), axis=0, keepdims=True), (SUB, HALF)
    )
    ref[HALF:TALL, HALF:BLK] = jnp.zeros((SUB, HALF), f32)


def unpacked(value):
    i, j = grids()
    cross, mixed, diagonal = value[0:HALF, 0:HALF], value[0:HALF, HALF:BLK], value[HALF : HALF + 1, 0:HALF]
    turned = mixed.T
    upper = jnp.where(i >= j, mixed, turned)
    lower = jnp.where(i < j, mixed, jnp.where(i > j, turned, diagonal))
    return upper, cross, lower


def gram_kernel(here_ref, acts_ref, out_ref, *, other):
    c = here_ref[2]
    first = (1 - c if other else c) * PER_CORE
    for k in range(PER_CORE):
        start = pl.multiple_of((first + k) * BLK, BLK)
        part = acts_ref[:, pl.ds(start, BLK)]
        total = lax.dot_general(part, part, (((0,), (0,)), ((), ())), preferred_element_type=f32)
        store_packed(
            out_ref.at[k], total[0:HALF, 0:HALF], total[HALF:BLK, 0:HALF], total[HALF:BLK, HALF:BLK]
        )


def parts_kernel(here_ref, mine_ref, got_ref, *out_refs):
    z, c = here_ref[1], here_ref[2]
    for step in range(N_Z):
        target = (z + step) % N_Z
        k = rank(target, c)

        @pl.when(holds(target, c))
        def _():
            out_refs[step][...] = mine_ref[k] + got_ref[k]


def small_inverse(d):
    d = dict(d)

    def at(i, j):
        return d[(i, j)] if i >= j else d[(j, i)]

    for k in range(SUB):
        inv = 1.0 / at(k, k)
        b = {i: at(i, k) * inv for i in range(SUB) if i != k}
        for i in b:
            for j in b:
                if j <= i:
                    d[(i, j)] = d[(i, j)] - b[i] * at(j, k)
        for i in b:
            d[(max(i, k), min(i, k))] = b[i]
        d[(k, k)] = -inv
    return d


def summed(terms):
    while len(terms) > 1:
        terms = [terms[n] + terms[n + 1] for n in range(0, len(terms), 2)]
    return terms[0]


def take_out(tiles, t):
    first = SUB * t
    lane = lax.broadcasted_iota(jnp.int32, (SUB, HALF), 1)
    line = lax.broadcasted_iota(jnp.int32, (SUB, HALF), 0)
    inside = (lane >= first) & (lane < first + SUB)
    pivot = tiles[t]

    def spread(v):
        return jnp.broadcast_to(v, (SUB, HALF))

    minus = small_inverse(
        {
            (i, j): spread(pivot[i : i + 1, first + j : first + j + 1])
            for i in range(SUB)
            for j in range(i + 1)
        }
    )
    rows = [
        jnp.where(lane == first + j, 1.0, jnp.where(inside, 0.0, spread(pivot[j : j + 1, :])))
        for j in range(SUB)
    ]
    new = [
        summed([minus[(max(i, j), min(i, j))] * rows[j] for j in range(SUB)]) for i in range(SUB)
    ]
    result = []
    for v, tile in enumerate(tiles):
        if v == t:
            own = jnp.zeros((SUB, HALF), f32)
            for j in range(SUB):
                own = jnp.where(line == j, -new[j], own)
            result.append(own)
        else:
            update = summed([spread(tile[:, first + j : first + j + 1]) * new[j] for j in range(SUB)])
            result.append(jnp.where(inside, 0.0, tile) + update)
    return result


def half_inverse(value):
    tiles = [value[SUB * v : SUB * v + SUB] for v in range(HALF // SUB)]
    for t in range(len(tiles)):
        tiles = take_out(tiles, t)
    return jnp.concatenate(tiles, axis=0)


def dot(a, b, dims=((1,), (0,))):
    return lax.dot_general(
        a, b, (dims, ((), ())), precision=lax.Precision.HIGHEST, preferred_element_type=f32
    )


def invert_kernel(here_ref, a_ref, b_ref, out_ref, *, all_tokens):
    z, c = here_ref[1], here_ref[2]

    @pl.when(holds(z, c))
    def _():
        upper, cross, lower = unpacked((a_ref[...] + b_ref[...]) * (1.0 / all_tokens))
        i, j = grids()
        same = i == j
        trace = jnp.sum(
            jnp.sum(jnp.where(same, upper + lower, 0.0), axis=0, keepdims=True), axis=1, keepdims=True
        )
        damping = damping_ratio * trace / BLK
        shift = jnp.where(same, damping, 0.0)
        first = half_inverse(upper + shift)
        w = dot(cross, first)
        second = half_inverse(lower + shift - dot(w, cross, ((1,), (1,))))
        x = dot(second, w)
        store_packed(out_ref, first + dot(w, x, ((0,), (0,))), -x, second)


def unpack_kernel(here_ref, *refs):
    in_refs, full_ref, rows_ref = refs[: 2 * N_Z], refs[2 * N_Z], refs[2 * N_Z + 1]
    x, z, c = here_ref[0], here_ref[1], here_ref[2]
    start = pl.multiple_of(((x * N_Z + z) * 2 + c) * SUB, SUB)
    for n, ref in enumerate(in_refs):
        core = c if n < N_Z else 1 - c
        source = (z + N_Z - n % N_Z) % N_Z
        block = core * PER_CORE + rank(source, core)

        @pl.when(holds(source, core))
        def _():
            upper, cross, lower = unpacked(ref[...])
            full_ref[block, 0:HALF, 0:HALF] = upper
            full_ref[block, 0:HALF, HALF:BLK] = cross.T
            full_ref[block, HALF:BLK, 0:HALF] = cross
            full_ref[block, HALF:BLK, HALF:BLK] = lower
            rows_ref[block] = full_ref[block, pl.ds(start, SUB), :]


def hosted_kernel(here_ref, owner_ref, rows_ref, out_ref):
    me = here_ref[3]
    out_ref[...] = jnp.zeros(out_ref.shape, f32)
    sections, nblocks = owner_ref.shape

    def section(s, count):
        for b in range(nblocks):
            mine = owner_ref[s, b] == me

            @pl.when(mine)
            def _(count=count):
                out_ref[count] = rows_ref[s, b]

            count = count + mine.astype(jnp.int32)
        return count

    lax.fori_loop(0, sections, section, jnp.int32(0))


def call(kernel, out_shape, n_smem, n_vmem):
    out_specs = jax.tree.map(lambda _: pl.BlockSpec(memory_space=VMEM), out_shape)
    return pl.pallas_call(
        kernel,
        out_shape=out_shape,
        in_specs=[pl.BlockSpec(memory_space=pltpu.SMEM)] * n_smem
        + [pl.BlockSpec(memory_space=VMEM)] * n_vmem,
        out_specs=out_specs,
        compiler_params=pltpu.CompilerParams(vmem_limit_bytes=40 * 1024 * 1024),
    )


def shape(*dims):
    return jax.ShapeDtypeStruct(dims, f32)


STEPS = (1, 7, 2, 6, 3, 5, 4)


def shards(acts, grad, owner_of):
    section_count = lax.axis_size("pipe")
    all_tokens = acts.shape[1] * lax.axis_size(DP)
    here = jnp.stack([lax.axis_index(a) for a in ("x", "z", "c", "pipe")]).astype(jnp.int32)
    features = acts[0]
    packed = shape(PER_CORE, TALL, BLK)
    theirs = call(functools.partial(gram_kernel, other=True), packed, 1, 1)(here, features)
    got = lax.ppermute(theirs, "c", [(0, 1), (1, 0)])
    mine = call(functools.partial(gram_kernel, other=False), packed, 1, 1)(here, features)
    parts = call(parts_kernel, [shape(TALL, BLK)] * N_Z, 1, 2)(here, mine, got)
    total = parts[0]
    arrived = [lax.ppermute(parts[step], ("z", "c"), place_of(step)[0]) for step in STEPS]
    for piece in arrived:
        total = total + piece
    other = lax.ppermute(total, "x", [(0, 1), (1, 0)])
    inverse = call(
        functools.partial(invert_kernel, all_tokens=all_tokens), shape(TALL, BLK), 1, 2
    )(here, total, other)
    near = {0: inverse}
    far = {0: lax.ppermute(inverse, "c", [(0, 1), (1, 0)])}
    for step in STEPS:
        near[step] = lax.ppermute(inverse, ("z", "c"), place_of(step)[1])
        far[step] = lax.ppermute(near[step], "c", [(0, 1), (1, 0)])
    gathered = [near[k] for k in range(N_Z)] + [far[k] for k in range(N_Z)]
    full, rows = call(unpack_kernel, [shape(NB, BLK, BLK), shape(NB, SUB, BLK)], 1, 2 * N_Z)(
        here, *gathered
    )
    everyone = lax.all_to_all(
        jnp.broadcast_to(rows[None], (section_count, *rows.shape)), "pipe", 0, 0, tiled=True
    )
    precond = jnp.einsum(
        "brk,bkc->brc", full, grad.reshape(NB, BLK, grad.shape[1]), precision=lax.Precision.HIGHEST
    )
    held = call(hosted_kernel, shape(HOST, SUB, BLK), 2, 1)(here, owner_of, everyone)
    return (precond.reshape(grad.shape), held[None])


def solution(mesh):
    torus = Mesh(mesh.devices.reshape(mesh.shape["pipe"], 2, N_Z, 2), ("pipe", "x", "z", "c"))
    placed = (P("pipe", DP, None), P("pipe", DP), P())
    return jax.shard_map(
        shards,
        mesh=torus,
        in_specs=placed,
        out_specs=(P("pipe", DP), P("pipe", None, DP, None)),
        check_vma=False,
    )
```

```python
import functools

import jax
import jax.numpy as jnp
from jax import lax
from jax.experimental import pallas as pl
from jax.experimental.pallas import tpu as pltpu
from jax.sharding import Mesh
from jax.sharding import PartitionSpec as P

BLK = 256
HALF = BLK // 2
SUB = 8
NB = 12
PER_CORE = NB // 2
HOST = 24
TALL = HALF + SUB
N_Z = 8
DP = ("x", "z", "c")
damping_ratio = 0.1
LIMIT = 8 * 1024 * 1024
VMEM = pltpu.VMEM
f32 = jnp.float32


def own_slot(here_ref):
    return (here_ref[1] + 4 * here_ref[0]) % N_Z


def holds(slot, c):
    return (slot % 4) != jnp.where(c == 0, 3, 1)


def rank(slot, c):
    return (slot // 4) * 3 + jnp.where(c == 0, slot % 4, (slot % 4 + 1) // 2)


OFFSETS = (0, 1, -1, 2, -2, 3, 4, 5)


def along_z(value, step):
    return lax.ppermute(value, "z", [(z, (z + step) % N_Z) for z in range(N_Z)])


def across_x(value):
    return lax.ppermute(value, "x", [(0, 1), (1, 0)])


def to_twin(value):
    pairs = [(x * N_Z + z, (1 - x) * N_Z + (z + 4) % N_Z) for x in range(2) for z in range(N_Z)]
    return lax.ppermute(value, ("x", "z"), pairs)


def across_cores(value):
    return lax.ppermute(value, "c", [(0, 1), (1, 0)])


def grids():
    return (
        lax.broadcasted_iota(jnp.int32, (HALF, HALF), 0),
        lax.broadcasted_iota(jnp.int32, (HALF, HALF), 1),
    )


def store_packed(ref, upper, cross, lower):
    i, j = grids()
    ref[0:HALF, 0:HALF] = cross
    ref[0:HALF, HALF:BLK] = jnp.where(i >= j, upper, lower)
    ref[HALF:TALL, 0:HALF] = jnp.broadcast_to(
        jnp.sum(jnp.where(i == j, lower, 0.0), axis=0, keepdims=True), (SUB, HALF)
    )
    ref[HALF:TALL, HALF:BLK] = jnp.zeros((SUB, HALF), f32)


def unpacked(value):
    i, j = grids()
    cross, mixed, diagonal = value[0:HALF, 0:HALF], value[0:HALF, HALF:BLK], value[HALF : HALF + 1, 0:HALF]
    turned = mixed.T
    upper = jnp.where(i >= j, mixed, turned)
    lower = jnp.where(i < j, mixed, jnp.where(i > j, turned, diagonal))
    return upper, cross, lower


def gram_kernel(here_ref, acts_ref, out_ref, *, other):
    c = here_ref[2]
    first = (1 - c if other else c) * PER_CORE
    for k in range(PER_CORE):
        start = pl.multiple_of((first + k) * BLK, BLK)
        part = acts_ref[:, pl.ds(start, BLK)]
        total = lax.dot_general(part, part, (((0,), (0,)), ((), ())), preferred_element_type=f32)
        store_packed(
            out_ref.at[k], total[0:HALF, 0:HALF], total[HALF:BLK, 0:HALF], total[HALF:BLK, HALF:BLK]
        )


def parts_kernel(here_ref, mine_ref, got_ref, *out_refs):
    c, own = here_ref[2], own_slot(here_ref)
    for offset, out_ref in zip(OFFSETS, out_refs):
        slot = (own + N_Z + offset) % N_Z
        k = rank(slot, c)

        @pl.when(holds(slot, c))
        def _():
            out_ref[...] = mine_ref[k] + got_ref[k]


def small_inverse(d):
    d = dict(d)

    def at(i, j):
        return d[(i, j)] if i >= j else d[(j, i)]

    for k in range(SUB):
        inv = 1.0 / at(k, k)
        b = {i: at(i, k) * inv for i in range(SUB) if i != k}
        for i in b:
            for j in b:
                if j <= i:
                    d[(i, j)] = d[(i, j)] - b[i] * at(j, k)
        for i in b:
            d[(max(i, k), min(i, k))] = b[i]
        d[(k, k)] = -inv
    return d


def summed(terms):
    while len(terms) > 1:
        terms = [terms[n] + terms[n + 1] for n in range(0, len(terms), 2)]
    return terms[0]


def take_out(tiles, t):
    first = SUB * t
    lane = lax.broadcasted_iota(jnp.int32, (SUB, HALF), 1)
    line = lax.broadcasted_iota(jnp.int32, (SUB, HALF), 0)
    inside = (lane >= first) & (lane < first + SUB)
    pivot = tiles[t]

    def spread(v):
        return jnp.broadcast_to(v, (SUB, HALF))

    minus = small_inverse(
        {
            (i, j): spread(pivot[i : i + 1, first + j : first + j + 1])
            for i in range(SUB)
            for j in range(i + 1)
        }
    )
    rows = [
        jnp.where(lane == first + j, 1.0, jnp.where(inside, 0.0, spread(pivot[j : j + 1, :])))
        for j in range(SUB)
    ]
    new = [
        summed([minus[(max(i, j), min(i, j))] * rows[j] for j in range(SUB)]) for i in range(SUB)
    ]
    result = []
    for v, tile in enumerate(tiles):
        if v == t:
            own = jnp.zeros((SUB, HALF), f32)
            for j in range(SUB):
                own = jnp.where(line == j, -new[j], own)
            result.append(own)
        else:
            update = summed([spread(tile[:, first + j : first + j + 1]) * new[j] for j in range(SUB)])
            result.append(jnp.where(inside, 0.0, tile) + update)
    return result


def half_inverse(value):
    tiles = [value[SUB * v : SUB * v + SUB] for v in range(HALF // SUB)]
    for t in range(len(tiles)):
        tiles = take_out(tiles, t)
    return jnp.concatenate(tiles, axis=0)


def dot(a, b, dims=((1,), (0,))):
    return lax.dot_general(
        a, b, (dims, ((), ())), precision=lax.Precision.HIGHEST, preferred_element_type=f32
    )


def invert_kernel(here_ref, a_ref, b_ref, out_ref, *, all_tokens):
    @pl.when(holds(own_slot(here_ref), here_ref[2]))
    def _():
        upper, cross, lower = unpacked((a_ref[...] + b_ref[...]) * (1.0 / all_tokens))
        i, j = grids()
        same = i == j
        trace = jnp.sum(
            jnp.sum(jnp.where(same, upper + lower, 0.0), axis=0, keepdims=True), axis=1, keepdims=True
        )
        damping = damping_ratio * trace / BLK
        shift = jnp.where(same, damping, 0.0)
        first = half_inverse(upper + shift)
        w = dot(cross, first)
        second = half_inverse(lower + shift - dot(w, cross, ((1,), (1,))))
        x = dot(second, w)
        store_packed(out_ref, first + dot(w, x, ((0,), (0,))), -x, second)


def unpack_blocks(here_ref, in_refs, full_ref, rows_ref, block_ref, done, *, other, first):
    c, own = here_ref[2], own_slot(here_ref)
    core = 1 - c if other else c
    start = pl.multiple_of(((here_ref[0] * N_Z + here_ref[1]) * 2 + c) * SUB, SUB)

    def leave(k):
        return pltpu.make_async_copy(block_ref.at[k], full_ref.at[core * PER_CORE + k], done.at[k])

    for offset, ref in zip(OFFSETS, in_refs):
        slot = (own + N_Z + offset) % N_Z
        k = rank(slot, core)

        @pl.when(holds(slot, core))
        def _():
            upper, cross, lower = unpacked(ref[...])
            block_ref[k, 0:HALF, 0:HALF] = upper
            block_ref[k, 0:HALF, HALF:BLK] = cross.T
            block_ref[k, HALF:BLK, 0:HALF] = cross
            block_ref[k, HALF:BLK, HALF:BLK] = lower
            leave(k).start()
            rows_ref[first + k] = block_ref[k, pl.ds(start, SUB), :]

    return [leave(k) for k in range(PER_CORE)]


def unpack_own_kernel(here_ref, *refs):
    full_ref, rows_ref, block_ref, done = refs[N_Z:]
    copies = unpack_blocks(
        here_ref, refs[:N_Z], full_ref, rows_ref, block_ref, done, other=False, first=0
    )
    for copy in copies:
        copy.wait()


def unpack_other_kernel(here_ref, *refs):
    own_rows_ref, _, full_ref, sent_ref, block_ref, rows_ref, done, gone = refs[N_Z:]
    c = here_ref[2]
    for k in range(PER_CORE):
        rows_ref[c * PER_CORE + k] = own_rows_ref[k]
    copies = unpack_blocks(
        here_ref, refs[:N_Z], full_ref, rows_ref, block_ref, done, other=True, first=(1 - c) * PER_CORE
    )
    sends = [
        pltpu.make_async_copy(rows_ref, sent_ref.at[s], gone.at[s]) for s in range(sent_ref.shape[0])
    ]
    for copy in sends:
        copy.start()
    for copy in copies + sends:
        copy.wait()


def precond_kernel(here_ref, owner_ref, full_ref, grad_ref, out_ref, table_ref):
    out_ref[...] = dot(full_ref[0], grad_ref[...])

    @pl.when(pl.program_id(0) == 0)
    def _():
        sections, nblocks = owner_ref.shape

        def clear(j, carry):
            table_ref[j] = -1
            return carry

        def section(s, count):
            for b in range(nblocks):
                hit = owner_ref[s, b] == here_ref[3]

                @pl.when(hit)
                def _(count=count):
                    table_ref[count] = s * nblocks + b

                count = count + hit.astype(jnp.int32)
            return count

        lax.fori_loop(0, HOST, clear, 0)
        lax.fori_loop(0, sections, section, jnp.int32(0))


def hosted_kernel(table_ref, rows_ref, out_ref):
    nblocks = rows_ref.shape[1]
    for j in range(HOST):
        source = table_ref[j]
        at = jnp.maximum(source, 0)
        rows = rows_ref[at // nblocks, at % nblocks]
        out_ref[j] = jnp.where(source >= 0, rows, 0.0)


def call(kernel, out_shape, n_smem, n_vmem):
    out_specs = jax.tree.map(lambda _: pl.BlockSpec(memory_space=VMEM), out_shape)
    return pl.pallas_call(
        kernel,
        out_shape=out_shape,
        in_specs=[pl.BlockSpec(memory_space=pltpu.SMEM)] * n_smem
        + [pl.BlockSpec(memory_space=VMEM)] * n_vmem,
        out_specs=out_specs,
        compiler_params=pltpu.CompilerParams(vmem_limit_bytes=LIMIT),
    )


def shape(*dims):
    return jax.ShapeDtypeStruct(dims, f32)


IN_HBM = pl.BlockSpec(memory_space=pltpu.HBM)
IN_VMEM = pl.BlockSpec(memory_space=VMEM)
IN_SMEM = pl.BlockSpec(memory_space=pltpu.SMEM)


def unpack_own(here, values):
    return pl.pallas_call(
        unpack_own_kernel,
        out_shape=[shape(NB, BLK, BLK), shape(PER_CORE, SUB, BLK)],
        in_specs=[IN_SMEM] + [IN_VMEM] * N_Z,
        out_specs=[IN_HBM, IN_VMEM],
        scratch_shapes=[VMEM((PER_CORE, BLK, BLK), f32), pltpu.SemaphoreType.DMA((PER_CORE,))],
        compiler_params=pltpu.CompilerParams(vmem_limit_bytes=LIMIT),
    )(here, *values)


def unpack_other(here, values, own_rows, full, copies):
    return pl.pallas_call(
        unpack_other_kernel,
        out_shape=[shape(NB, BLK, BLK), shape(copies, NB, SUB, BLK)],
        in_specs=[IN_SMEM] + [IN_VMEM] * (N_Z + 1) + [IN_HBM],
        out_specs=[IN_HBM, IN_HBM],
        scratch_shapes=[
            VMEM((PER_CORE, BLK, BLK), f32),
            VMEM((NB, SUB, BLK), f32),
            pltpu.SemaphoreType.DMA((PER_CORE,)),
            pltpu.SemaphoreType.DMA((copies,)),
        ],
        input_output_aliases={2 + N_Z: 0},
        compiler_params=pltpu.CompilerParams(vmem_limit_bytes=LIMIT),
    )(here, *values, own_rows, full)


def preconditioned(here, owner_of, full, grad):
    rows, columns = grad.shape
    part = pl.BlockSpec((BLK, columns), lambda i: (i, 0))
    scalars = pl.BlockSpec(memory_space=pltpu.SMEM)
    return pl.pallas_call(
        precond_kernel,
        grid=(rows // BLK,),
        out_shape=[shape(rows, columns), jax.ShapeDtypeStruct((HOST,), jnp.int32)],
        in_specs=[scalars, scalars, pl.BlockSpec((1, BLK, BLK), lambda i: (i, 0, 0)), part],
        out_specs=[part, scalars],
        cost_estimate=pl.CostEstimate(
            flops=12 * rows * BLK * columns, bytes_accessed=16 * rows * columns, transcendentals=0
        ),
        compiler_params=pltpu.CompilerParams(vmem_limit_bytes=LIMIT),
    )(here, owner_of, full, grad)


def shards(acts, grad, owner_of):
    section_count = lax.axis_size("pipe")
    all_tokens = acts.shape[1] * lax.axis_size(DP)
    here = jnp.stack([lax.axis_index(a) for a in ("x", "z", "c", "pipe")]).astype(jnp.int32)
    features = acts[0]
    packed = shape(PER_CORE, TALL, BLK)
    one = shape(TALL, BLK)
    theirs = call(functools.partial(gram_kernel, other=True), packed, 1, 1)(here, features)
    got = across_cores(theirs)
    mine = call(functools.partial(gram_kernel, other=False), packed, 1, 1)(here, features)
    part = dict(zip(OFFSETS, call(parts_kernel, [one] * N_Z, 1, 2)(here, mine, got)))

    across = {1: across_x(part[5]), -1: across_x(part[3])}
    far = [along_z(part[2], 2), along_z(part[-2], -2)]
    across[0] = across_x(part[4])
    near = [along_z(part[1] + across[1], 1), along_z(part[-1] + across[-1], -1)]
    half = part[0] + across[0] + far[0] + far[1] + near[0] + near[1]
    other_half = to_twin(half)
    inverse = call(functools.partial(invert_kernel, all_tokens=all_tokens), one, 1, 2)(
        here, half, other_half
    )

    held = {0: inverse, -1: along_z(inverse, 1), 1: along_z(inverse, -1)}
    held[4] = across_x(inverse)
    held[-2], held[2] = along_z(inverse, 2), along_z(inverse, -2)
    held[3], held[5] = across_x(held[-1]), across_x(held[1])
    gathered = lax.optimization_barrier([held[k] for k in OFFSETS])
    passed = [across_cores(value) for value in gathered]
    full, own_rows = unpack_own(here, gathered)
    full, sent = unpack_other(here, passed, own_rows, full, section_count)
    everyone = lax.all_to_all(sent, "pipe", 0, 0, tiled=True)
    precond, table = preconditioned(here, owner_of, full, grad)
    hosted = call(hosted_kernel, shape(HOST, SUB, BLK), 1, 1)(table, everyone)
    return (precond, hosted[None])


def solution(mesh):
    torus = Mesh(mesh.devices.reshape(mesh.shape["pipe"], 2, N_Z, 2), ("pipe", "x", "z", "c"))
    placed = (P("pipe", DP, None), P("pipe", DP), P())
    return jax.shard_map(
        shards,
        mesh=torus,
        in_specs=placed,
        out_specs=(P("pipe", DP), P("pipe", None, DP, None)),
        check_vma=False,
    )
```

```python
import functools

import jax
import jax.numpy as jnp
from jax import lax
from jax.experimental import pallas as pl
from jax.experimental.pallas import tpu as pltpu
from jax.sharding import Mesh
from jax.sharding import PartitionSpec as P

BLK = 256
HALF = BLK // 2
SUB = 8
NB = 12
PER_CORE = NB // 2
HOST = 24
TALL = HALF + SUB
N_Z = 8
DP = ("x", "z", "c")
damping_ratio = 0.1
LIMIT = 8 * 1024 * 1024
ALMOST_ALL = 65 * 1000 * 1000
VMEM = pltpu.VMEM
f32 = jnp.float32


def own_slot(here_ref):
    return (here_ref[1] + 4 * here_ref[0]) % N_Z


def holds(slot, c):
    return (slot % 4) != jnp.where(c == 0, 3, 1)


def rank(slot, c):
    return (slot // 4) * 3 + jnp.where(c == 0, slot % 4, (slot % 4 + 1) // 2)


OFFSETS = (0, 1, -1, 2, -2, 3, 4, 5)


def along_z(value, step):
    return lax.ppermute(value, "z", [(z, (z + step) % N_Z) for z in range(N_Z)])


def across_x(value):
    return lax.ppermute(value, "x", [(0, 1), (1, 0)])


def to_twin(value):
    pairs = [(x * N_Z + z, (1 - x) * N_Z + (z + 4) % N_Z) for x in range(2) for z in range(N_Z)]
    return lax.ppermute(value, ("x", "z"), pairs)


def across_cores(value):
    return lax.ppermute(value, "c", [(0, 1), (1, 0)])


def grids():
    return (
        lax.broadcasted_iota(jnp.int32, (HALF, HALF), 0),
        lax.broadcasted_iota(jnp.int32, (HALF, HALF), 1),
    )


def store_packed(ref, upper, cross, lower):
    i, j = grids()
    ref[0:HALF, 0:HALF] = cross
    ref[0:HALF, HALF:BLK] = jnp.where(i >= j, upper, lower)
    ref[HALF:TALL, 0:HALF] = jnp.broadcast_to(
        jnp.sum(jnp.where(i == j, lower, 0.0), axis=0, keepdims=True), (SUB, HALF)
    )
    ref[HALF:TALL, HALF:BLK] = jnp.zeros((SUB, HALF), f32)


def unpacked(value):
    i, j = grids()
    cross, mixed, diagonal = value[0:HALF, 0:HALF], value[0:HALF, HALF:BLK], value[HALF : HALF + 1, 0:HALF]
    turned = mixed.T
    upper = jnp.where(i >= j, mixed, turned)
    lower = jnp.where(i < j, mixed, jnp.where(i > j, turned, diagonal))
    return upper, cross, lower


def gram_kernel(here_ref, acts_ref, out_ref, part_ref, got, *, other):
    c = here_ref[2]
    first = (1 - c if other else c) * PER_CORE

    def fetch(k):
        columns = pl.ds(pl.multiple_of((first + k) * BLK, BLK), BLK)
        return pltpu.make_async_copy(acts_ref.at[:, columns], part_ref.at[k], got.at[k])

    for k in range(PER_CORE):
        fetch(k).start()
    for k in range(PER_CORE):
        fetch(k).wait()
        part = part_ref[k]
        total = lax.dot_general(part, part, (((0,), (0,)), ((), ())), preferred_element_type=f32)
        store_packed(
            out_ref.at[k], total[0:HALF, 0:HALF], total[HALF:BLK, 0:HALF], total[HALF:BLK, HALF:BLK]
        )


def parts_kernel(here_ref, mine_ref, got_ref, *out_refs):
    c, own = here_ref[2], own_slot(here_ref)
    for offset, out_ref in zip(OFFSETS, out_refs):
        slot = (own + N_Z + offset) % N_Z
        k = rank(slot, c)

        @pl.when(holds(slot, c))
        def _():
            out_ref[...] = mine_ref[k] + got_ref[k]


def small_inverse(d):
    d = dict(d)

    def at(i, j):
        return d[(i, j)] if i >= j else d[(j, i)]

    for k in range(SUB):
        inv = 1.0 / at(k, k)
        b = {i: at(i, k) * inv for i in range(SUB) if i != k}
        for i in b:
            for j in b:
                if j <= i:
                    d[(i, j)] = d[(i, j)] - b[i] * at(j, k)
        for i in b:
            d[(max(i, k), min(i, k))] = b[i]
        d[(k, k)] = -inv
    return d


def summed(terms):
    while len(terms) > 1:
        terms = [terms[n] + terms[n + 1] for n in range(0, len(terms), 2)]
    return terms[0]


def take_out(tiles, t):
    first = SUB * t
    lane = lax.broadcasted_iota(jnp.int32, (SUB, HALF), 1)
    line = lax.broadcasted_iota(jnp.int32, (SUB, HALF), 0)
    inside = (lane >= first) & (lane < first + SUB)
    pivot = tiles[t]

    def spread(v):
        return jnp.broadcast_to(v, (SUB, HALF))

    minus = small_inverse(
        {
            (i, j): spread(pivot[i : i + 1, first + j : first + j + 1])
            for i in range(SUB)
            for j in range(i + 1)
        }
    )
    rows = [
        jnp.where(lane == first + j, 1.0, jnp.where(inside, 0.0, spread(pivot[j : j + 1, :])))
        for j in range(SUB)
    ]
    new = [
        summed([minus[(max(i, j), min(i, j))] * rows[j] for j in range(SUB)]) for i in range(SUB)
    ]
    result = []
    for v, tile in enumerate(tiles):
        if v == t:
            own = jnp.zeros((SUB, HALF), f32)
            for j in range(SUB):
                own = jnp.where(line == j, -new[j], own)
            result.append(own)
        else:
            update = summed([spread(tile[:, first + j : first + j + 1]) * new[j] for j in range(SUB)])
            result.append(jnp.where(inside, 0.0, tile) + update)
    return result


def half_inverse(value):
    tiles = [value[SUB * v : SUB * v + SUB] for v in range(HALF // SUB)]
    for t in range(len(tiles)):
        tiles = take_out(tiles, t)
    return jnp.concatenate(tiles, axis=0)


def dot(a, b, dims=((1,), (0,))):
    return lax.dot_general(
        a, b, (dims, ((), ())), precision=lax.Precision.HIGHEST, preferred_element_type=f32
    )


def invert_kernel(here_ref, a_ref, b_ref, out_ref, *, all_tokens):
    @pl.when(holds(own_slot(here_ref), here_ref[2]))
    def _():
        upper, cross, lower = unpacked((a_ref[...] + b_ref[...]) * (1.0 / all_tokens))
        i, j = grids()
        same = i == j
        trace = jnp.sum(
            jnp.sum(jnp.where(same, upper + lower, 0.0), axis=0, keepdims=True), axis=1, keepdims=True
        )
        damping = damping_ratio * trace / BLK
        shift = jnp.where(same, damping, 0.0)
        first = half_inverse(upper + shift)
        w = dot(cross, first)
        second = half_inverse(lower + shift - dot(w, cross, ((1,), (1,))))
        x = dot(second, w)
        store_packed(out_ref, first + dot(w, x, ((0,), (0,))), -x, second)


def unpack_kernel(here_ref, *refs):
    in_refs, (full_ref, mine_ref, theirs_ref) = refs[:N_Z], refs[N_Z:]
    c, own = here_ref[2], own_slot(here_ref)
    start = (here_ref[0] * N_Z + here_ref[1]) * 2

    def rows(k, core):
        return full_ref[k, pl.ds(pl.multiple_of((start + core) * SUB, SUB), SUB), :]

    for offset, ref in zip(OFFSETS, in_refs):
        slot = (own + N_Z + offset) % N_Z
        k = rank(slot, c)

        @pl.when(holds(slot, c))
        def _():
            upper, cross, lower = unpacked(ref[...])
            full_ref[k, 0:HALF, 0:HALF] = upper
            full_ref[k, 0:HALF, HALF:BLK] = cross.T
            full_ref[k, HALF:BLK, 0:HALF] = cross
            full_ref[k, HALF:BLK, HALF:BLK] = lower
            mine_ref[k] = rows(k, c)
            theirs_ref[k] = rows(k, 1 - c)


def spread_kernel(here_ref, own_ref, other_ref, out_ref):
    c = here_ref[2]
    for k in range(PER_CORE):
        own, other = own_ref[k], other_ref[k]
        for s in range(out_ref.shape[0]):
            out_ref[s, c * PER_CORE + k] = own
            out_ref[s, (1 - c) * PER_CORE + k] = other


def precond_kernel(here_ref, owner_ref, own_ref, other_ref, grad_ref, out_ref, pick_ref, table_ref):
    step = pl.program_id(0)
    k = step % PER_CORE

    @pl.when(step < PER_CORE)
    def _():
        out_ref[...] = dot(own_ref[k], grad_ref[...])

    @pl.when(step >= PER_CORE)
    def _():
        out_ref[...] = dot(other_ref[k], grad_ref[...])

    @pl.when(step == 0)
    def _():
        sections, nblocks = owner_ref.shape
        for j in range(HOST):
            table_ref[j] = -1

        def section(s, count):
            for b in range(nblocks):
                hit = owner_ref[s, b] == here_ref[3]

                @pl.when(hit)
                def _(count=count):
                    table_ref[count] = s * nblocks + b

                count = count + hit.astype(jnp.int32)
            return count

        lax.fori_loop(0, sections, section, jnp.int32(0))
        block = lax.broadcasted_iota(jnp.int32, (1, sections * nblocks), 1)
        for j in range(HOST):
            pick_ref[j : j + 1, :] = (block == table_ref[j]).astype(f32)


def call(kernel, out_shape, n_smem, n_vmem):
    out_specs = jax.tree.map(lambda _: pl.BlockSpec(memory_space=VMEM), out_shape)
    return pl.pallas_call(
        kernel,
        out_shape=out_shape,
        in_specs=[pl.BlockSpec(memory_space=pltpu.SMEM)] * n_smem
        + [pl.BlockSpec(memory_space=VMEM)] * n_vmem,
        out_specs=out_specs,
        compiler_params=pltpu.CompilerParams(vmem_limit_bytes=LIMIT),
    )


def shape(*dims):
    return jax.ShapeDtypeStruct(dims, f32)


IN_VMEM = pl.BlockSpec(memory_space=VMEM)
IN_SMEM = pl.BlockSpec(memory_space=pltpu.SMEM)


def grams(here, features, other):
    return pl.pallas_call(
        functools.partial(gram_kernel, other=other),
        out_shape=shape(PER_CORE, TALL, BLK),
        in_specs=[IN_SMEM, pl.BlockSpec(memory_space=pl.ANY)],
        out_specs=IN_VMEM,
        scratch_shapes=[
            VMEM((PER_CORE, features.shape[0], BLK), features.dtype),
            pltpu.SemaphoreType.DMA((PER_CORE,)),
        ],
        compiler_params=pltpu.CompilerParams(vmem_limit_bytes=ALMOST_ALL if other else LIMIT),
    )(here, features)


def preconditioned(here, owner_of, own, other, grad):
    rows, columns = grad.shape

    def block(i, here_ref):
        c = here_ref[2]
        return jnp.where(i < PER_CORE, c * PER_CORE + i, (1 - c) * PER_CORE + i - PER_CORE), 0

    part = pl.BlockSpec((BLK, columns), block)
    pick = shape(HOST, owner_of.size)
    return pl.pallas_call(
        precond_kernel,
        grid_spec=pltpu.PrefetchScalarGridSpec(
            num_scalar_prefetch=1,
            grid=(rows // BLK,),
            in_specs=[IN_SMEM, IN_VMEM, IN_VMEM, part],
            out_specs=[part, pl.BlockSpec(pick.shape, lambda i, here_ref: (0, 0))],
            scratch_shapes=[pltpu.SMEM((HOST,), jnp.int32)],
        ),
        out_shape=[shape(rows, columns), pick],
        cost_estimate=pl.CostEstimate(
            flops=12 * rows * BLK * columns, bytes_accessed=16 * rows * columns, transcendentals=0
        ),
        compiler_params=pltpu.CompilerParams(vmem_limit_bytes=LIMIT),
    )(here, owner_of, own, other, grad)


def shards(acts, grad, owner_of):
    section_count = lax.axis_size("pipe")
    all_tokens = acts.shape[1] * lax.axis_size(DP)
    here = jnp.stack([lax.axis_index(a) for a in ("x", "z", "c", "pipe")]).astype(jnp.int32)
    features = acts[0]
    one = shape(TALL, BLK)
    got = across_cores(grams(here, features, True))
    mine = grams(here, features, False)
    part = dict(zip(OFFSETS, call(parts_kernel, [one] * N_Z, 1, 2)(here, mine, got)))

    across = {1: across_x(part[5]), -1: across_x(part[3])}
    far = [along_z(part[2], 2), along_z(part[-2], -2)]
    across[0] = across_x(part[4])
    near = [along_z(part[1] + across[1], 1), along_z(part[-1] + across[-1], -1)]
    half = part[0] + across[0] + far[0] + far[1] + near[0] + near[1]
    other_half = to_twin(half)
    inverse = call(functools.partial(invert_kernel, all_tokens=all_tokens), one, 1, 2)(
        here, half, other_half
    )

    held = {0: inverse, -1: along_z(inverse, 1), 1: along_z(inverse, -1)}
    held[4] = across_x(inverse)
    held[-2], held[2] = along_z(inverse, 2), along_z(inverse, -2)
    held[3], held[5] = across_x(held[-1]), across_x(held[1])
    opened = [shape(PER_CORE, BLK, BLK)] + [shape(PER_CORE, SUB, BLK)] * 2
    own, own_rows, their_rows = call(unpack_kernel, opened, 1, N_Z)(here, *[held[k] for k in OFFSETS])
    other_rows = across_cores(their_rows)
    other = across_cores(own)
    sent = call(spread_kernel, shape(section_count, NB, SUB, BLK), 1, 2)(here, own_rows, other_rows)
    everyone = lax.all_to_all(sent, "pipe", 0, 0, tiled=True)
    precond, pick = preconditioned(here, owner_of, own, other, grad)
    hosted = jnp.einsum(
        "jk,krc->jrc", pick, everyone.reshape(-1, SUB, BLK), precision=lax.Precision.HIGHEST
    )
    return (precond, hosted[None])


def solution(mesh):
    torus = Mesh(mesh.devices.reshape(mesh.shape["pipe"], 2, N_Z, 2), ("pipe", "x", "z", "c"))
    placed = (P("pipe", DP, None), P("pipe", DP), P())
    return jax.shard_map(
        shards,
        mesh=torus,
        in_specs=placed,
        out_specs=(P("pipe", DP), P("pipe", None, DP, None)),
        check_vma=False,
    )
```

```python
import functools

import jax
import jax.numpy as jnp
from jax import lax
from jax.experimental import pallas as pl
from jax.experimental.pallas import tpu as pltpu
from jax.sharding import Mesh
from jax.sharding import PartitionSpec as P

BLK = 256
HALF = BLK // 2
SUB = 8
NB = 12
PER_CORE = NB // 2
HOST = 24
TALL = HALF + SUB
N_Z = 8
DP = ("x", "z", "c")
damping_ratio = 0.1
LIMIT = 8 * 1024 * 1024
VMEM = pltpu.VMEM
f32 = jnp.float32


def own_slot(here_ref):
    return (here_ref[1] + 4 * here_ref[0]) % N_Z


def holds(slot, c):
    return (slot % 4) != jnp.where(c == 0, 3, 1)


def rank(slot, c):
    return (slot // 4) * 3 + jnp.where(c == 0, slot % 4, (slot % 4 + 1) // 2)


OFFSETS = (0, 1, -1, 2, -2, 3, 4, 5)
PAIR = (5, 3)


def along_z(value, step):
    return lax.ppermute(value, "z", [(z, (z + step) % N_Z) for z in range(N_Z)])


def across_x(value):
    return lax.ppermute(value, "x", [(0, 1), (1, 0)])


def to_twin(value):
    pairs = [(x * N_Z + z, (1 - x) * N_Z + (z + 4) % N_Z) for x in range(2) for z in range(N_Z)]
    return lax.ppermute(value, ("x", "z"), pairs)


def across_cores(value):
    return lax.ppermute(value, "c", [(0, 1), (1, 0)])


def grids():
    return (
        lax.broadcasted_iota(jnp.int32, (HALF, HALF), 0),
        lax.broadcasted_iota(jnp.int32, (HALF, HALF), 1),
    )


def store_packed(ref, upper, cross, lower):
    i, j = grids()
    ref[0:HALF, 0:HALF] = cross
    ref[0:HALF, HALF:BLK] = jnp.where(i >= j, upper, lower)
    ref[HALF:TALL, 0:HALF] = jnp.broadcast_to(
        jnp.sum(jnp.where(i == j, lower, 0.0), axis=0, keepdims=True), (SUB, HALF)
    )
    ref[HALF:TALL, HALF:BLK] = jnp.zeros((SUB, HALF), f32)


def unpacked(value):
    i, j = grids()
    cross, mixed, diagonal = value[0:HALF, 0:HALF], value[0:HALF, HALF:BLK], value[HALF : HALF + 1, 0:HALF]
    turned = mixed.T
    upper = jnp.where(i >= j, mixed, turned)
    lower = jnp.where(i < j, mixed, jnp.where(i > j, turned, diagonal))
    return upper, cross, lower


def gram_kernel(here_ref, acts_ref, out_ref, *, other):
    c = here_ref[2]
    first = (1 - c if other else c) * PER_CORE
    for k in range(PER_CORE):
        start = pl.multiple_of((first + k) * BLK, BLK)
        part = acts_ref[:, pl.ds(start, BLK)]
        total = lax.dot_general(part, part, (((0,), (0,)), ((), ())), preferred_element_type=f32)
        store_packed(
            out_ref.at[k], total[0:HALF, 0:HALF], total[HALF:BLK, 0:HALF], total[HALF:BLK, HALF:BLK]
        )


def parts_kernel(here_ref, mine_ref, got_ref, pair_ref, *out_refs):
    c, own = here_ref[2], own_slot(here_ref)
    single = [offset for offset in OFFSETS if offset not in PAIR]
    targets = [(offset, pair_ref.at[n]) for n, offset in enumerate(PAIR)] + list(zip(single, out_refs))
    for offset, out_ref in targets:
        slot = (own + N_Z + offset) % N_Z
        k = rank(slot, c)

        @pl.when(holds(slot, c))
        def _():
            out_ref[...] = mine_ref[k] + got_ref[k]


def small_inverse(d):
    d = dict(d)

    def at(i, j):
        return d[(i, j)] if i >= j else d[(j, i)]

    for k in range(SUB):
        inv = 1.0 / at(k, k)
        b = {i: at(i, k) * inv for i in range(SUB) if i != k}
        for i in b:
            for j in b:
                if j <= i:
                    d[(i, j)] = d[(i, j)] - b[i] * at(j, k)
        for i in b:
            d[(max(i, k), min(i, k))] = b[i]
        d[(k, k)] = -inv
    return d


def summed(terms):
    while len(terms) > 1:
        terms = [terms[n] + terms[n + 1] for n in range(0, len(terms), 2)]
    return terms[0]


def take_out(tiles, t):
    first = SUB * t
    lane = lax.broadcasted_iota(jnp.int32, (SUB, HALF), 1)
    line = lax.broadcasted_iota(jnp.int32, (SUB, HALF), 0)
    inside = (lane >= first) & (lane < first + SUB)
    pivot = tiles[t]

    def spread(v):
        return jnp.broadcast_to(v, (SUB, HALF))

    minus = small_inverse(
        {
            (i, j): spread(pivot[i : i + 1, first + j : first + j + 1])
            for i in range(SUB)
            for j in range(i + 1)
        }
    )
    rows = [
        jnp.where(lane == first + j, 1.0, jnp.where(inside, 0.0, spread(pivot[j : j + 1, :])))
        for j in range(SUB)
    ]
    new = [
        summed([minus[(max(i, j), min(i, j))] * rows[j] for j in range(SUB)]) for i in range(SUB)
    ]
    result = []
    for v, tile in enumerate(tiles):
        if v == t:
            own = jnp.zeros((SUB, HALF), f32)
            for j in range(SUB):
                own = jnp.where(line == j, -new[j], own)
            result.append(own)
        else:
            update = summed([spread(tile[:, first + j : first + j + 1]) * new[j] for j in range(SUB)])
            result.append(jnp.where(inside, 0.0, tile) + update)
    return result


def half_inverse(value):
    tiles = [value[SUB * v : SUB * v + SUB] for v in range(HALF // SUB)]
    for t in range(len(tiles)):
        tiles = take_out(tiles, t)
    return jnp.concatenate(tiles, axis=0)


def dot(a, b, dims=((1,), (0,))):
    return lax.dot_general(
        a, b, (dims, ((), ())), precision=lax.Precision.HIGHEST, preferred_element_type=f32
    )


def invert_kernel(here_ref, a_ref, b_ref, out_ref, *, all_tokens):
    @pl.when(holds(own_slot(here_ref), here_ref[2]))
    def _():
        upper, cross, lower = unpacked((a_ref[...] + b_ref[...]) * (1.0 / all_tokens))
        i, j = grids()
        same = i == j
        trace = jnp.sum(
            jnp.sum(jnp.where(same, upper + lower, 0.0), axis=0, keepdims=True), axis=1, keepdims=True
        )
        damping = damping_ratio * trace / BLK
        shift = jnp.where(same, damping, 0.0)
        first = half_inverse(upper + shift)
        w = dot(cross, first)
        second = half_inverse(lower + shift - dot(w, cross, ((1,), (1,))))
        x = dot(second, w)
        store_packed(out_ref, first + dot(w, x, ((0,), (0,))), -x, second)


def unpack_kernel(here_ref, *refs):
    in_refs, (full_ref, mine_ref, theirs_ref) = refs[:N_Z], refs[N_Z:]
    c, own = here_ref[2], own_slot(here_ref)
    start = (here_ref[0] * N_Z + here_ref[1]) * 2

    def rows(k, core):
        return full_ref[k, pl.ds(pl.multiple_of((start + core) * SUB, SUB), SUB), :]

    for offset, ref in zip(OFFSETS, in_refs):
        slot = (own + N_Z + offset) % N_Z
        k = rank(slot, c)

        @pl.when(holds(slot, c))
        def _():
            upper, cross, lower = unpacked(ref[...])
            full_ref[k, 0:HALF, 0:HALF] = upper
            full_ref[k, 0:HALF, HALF:BLK] = cross.T
            full_ref[k, HALF:BLK, 0:HALF] = cross
            full_ref[k, HALF:BLK, HALF:BLK] = lower
            mine_ref[k] = rows(k, c)
            theirs_ref[k] = rows(k, 1 - c)


def precond_kernel(here_ref, owner_ref, own_ref, other_ref, grad_ref, out_ref, table_ref):
    step = pl.program_id(0)
    k = step % PER_CORE

    @pl.when(step < PER_CORE)
    def _():
        out_ref[...] = dot(own_ref[k], grad_ref[...])

    @pl.when(step >= PER_CORE)
    def _():
        out_ref[...] = dot(other_ref[k], grad_ref[...])

    @pl.when(step == 0)
    def _():
        sections, nblocks = owner_ref.shape
        for j in range(HOST):
            table_ref[j] = -1

        def section(s, count):
            for b in range(nblocks):
                hit = owner_ref[s, b] == here_ref[3]

                @pl.when(hit)
                def _(count=count):
                    table_ref[count] = s * nblocks + (b + here_ref[2] * PER_CORE) % nblocks

                count = count + hit.astype(jnp.int32)
            return count

        lax.fori_loop(0, sections, section, jnp.int32(0))


def hosted_kernel(table_ref, rows_ref, out_ref):
    nblocks = rows_ref.shape[1]
    for j in range(HOST):
        source = table_ref[j]
        at = jnp.maximum(source, 0)
        rows = rows_ref[at // nblocks, at % nblocks]
        out_ref[j] = jnp.where(source >= 0, rows, 0.0)


def call(kernel, out_shape, n_smem, n_vmem):
    out_specs = jax.tree.map(lambda _: pl.BlockSpec(memory_space=VMEM), out_shape)
    return pl.pallas_call(
        kernel,
        out_shape=out_shape,
        in_specs=[pl.BlockSpec(memory_space=pltpu.SMEM)] * n_smem
        + [pl.BlockSpec(memory_space=VMEM)] * n_vmem,
        out_specs=out_specs,
        compiler_params=pltpu.CompilerParams(vmem_limit_bytes=LIMIT),
    )


def shape(*dims):
    return jax.ShapeDtypeStruct(dims, f32)


IN_VMEM = pl.BlockSpec(memory_space=VMEM)
IN_SMEM = pl.BlockSpec(memory_space=pltpu.SMEM)


def preconditioned(here, owner_of, own, other, grad):
    rows, columns = grad.shape

    def block(i, here_ref):
        c = here_ref[2]
        return jnp.where(i < PER_CORE, c * PER_CORE + i, (1 - c) * PER_CORE + i - PER_CORE), 0

    part = pl.BlockSpec((BLK, columns), block)
    return pl.pallas_call(
        precond_kernel,
        grid_spec=pltpu.PrefetchScalarGridSpec(
            num_scalar_prefetch=1,
            grid=(rows // BLK,),
            in_specs=[IN_SMEM, IN_VMEM, IN_VMEM, part],
            out_specs=[part, IN_SMEM],
        ),
        out_shape=[shape(rows, columns), jax.ShapeDtypeStruct((HOST,), jnp.int32)],
        cost_estimate=pl.CostEstimate(
            flops=12 * rows * BLK * columns, bytes_accessed=16 * rows * columns, transcendentals=0
        ),
        compiler_params=pltpu.CompilerParams(vmem_limit_bytes=LIMIT),
    )(here, owner_of, own, other, grad)


def shards(acts, grad, owner_of):
    section_count = lax.axis_size("pipe")
    all_tokens = acts.shape[1] * lax.axis_size(DP)
    here = jnp.stack([lax.axis_index(a) for a in ("x", "z", "c", "pipe")]).astype(jnp.int32)
    features = acts[0]
    one = shape(TALL, BLK)
    packed = shape(PER_CORE, TALL, BLK)
    got = across_cores(call(functools.partial(gram_kernel, other=True), packed, 1, 1)(here, features))
    mine = call(functools.partial(gram_kernel, other=False), packed, 1, 1)(here, features)
    single = [offset for offset in OFFSETS if offset not in PAIR]
    parts = call(parts_kernel, [shape(2, TALL, BLK)] + [one] * len(single), 1, 2)(here, mine, got)
    part = dict(zip(single, parts[1:]))

    pair = across_x(parts[0])
    far = [along_z(part[2], 2), along_z(part[-2], -2)]
    across = across_x(part[4])
    near = [along_z(part[1] + pair[0], 1), along_z(part[-1] + pair[1], -1)]
    half = part[0] + across + far[0] + far[1] + near[0] + near[1]
    other_half = to_twin(half)
    inverse = call(functools.partial(invert_kernel, all_tokens=all_tokens), one, 1, 2)(
        here, half, other_half
    )

    held = {0: inverse, -1: along_z(inverse, 1), 1: along_z(inverse, -1)}
    held[4] = across_x(inverse)
    held[-2], held[2] = along_z(inverse, 2), along_z(inverse, -2)
    held[3], held[5] = across_x(held[-1]), across_x(held[1])
    opened = [shape(PER_CORE, BLK, BLK)] + [shape(PER_CORE, SUB, BLK)] * 2
    own, own_rows, their_rows = call(unpack_kernel, opened, 1, N_Z)(here, *[held[k] for k in OFFSETS])
    other_rows = across_cores(their_rows)
    rows = jnp.concatenate([own_rows, other_rows])
    sent = jnp.broadcast_to(rows[None], (section_count, *rows.shape))
    own, sent = lax.optimization_barrier((own, sent))
    other = across_cores(own)
    everyone = lax.all_to_all(sent, "pipe", 0, 0, tiled=True)
    precond, table = preconditioned(here, owner_of, own, other, grad)
    hosted = call(hosted_kernel, shape(HOST, SUB, BLK), 1, 1)(table, everyone)
    return (precond, hosted[None])


def solution(mesh):
    torus = Mesh(mesh.devices.reshape(mesh.shape["pipe"], 2, N_Z, 2), ("pipe", "x", "z", "c"))
    placed = (P("pipe", DP, None), P("pipe", DP), P())
    return jax.shard_map(
        shards,
        mesh=torus,
        in_specs=placed,
        out_specs=(P("pipe", DP), P("pipe", None, DP, None)),
        check_vma=False,
    )
```

```python
import functools

import jax
import jax.numpy as jnp
from jax import lax
from jax.experimental import pallas as pl
from jax.experimental.pallas import tpu as pltpu
from jax.sharding import Mesh
from jax.sharding import PartitionSpec as P

BLK = 256
HALF = BLK // 2
SUB = 8
NB = 12
PER_CORE = NB // 2
HOST = 24
TALL = HALF + SUB
N_Z = 8
DP = ("x", "z", "c")
damping_ratio = 0.1
LIMIT = 8 * 1024 * 1024
VMEM = pltpu.VMEM
f32 = jnp.float32


def own_slot(here_ref):
    return (here_ref[1] + 4 * here_ref[0]) % N_Z


def holds(slot, c):
    return (slot % 4) != jnp.where(c == 0, 3, 1)


def rank(slot, c):
    return (slot // 4) * 3 + jnp.where(c == 0, slot % 4, (slot % 4 + 1) // 2)


OFFSETS = (0, 1, -1, 2, -2, 3, 4, 5)
PAIR = (5, 3)


def along_z(value, step):
    return lax.ppermute(value, "z", [(z, (z + step) % N_Z) for z in range(N_Z)])


def across_x(value):
    return lax.ppermute(value, "x", [(0, 1), (1, 0)])


def to_twin(value):
    pairs = [(x * N_Z + z, (1 - x) * N_Z + (z + 4) % N_Z) for x in range(2) for z in range(N_Z)]
    return lax.ppermute(value, ("x", "z"), pairs)


def across_cores(value):
    return lax.ppermute(value, "c", [(0, 1), (1, 0)])


def grids():
    return (
        lax.broadcasted_iota(jnp.int32, (HALF, HALF), 0),
        lax.broadcasted_iota(jnp.int32, (HALF, HALF), 1),
    )


def store_packed(ref, upper, cross, lower):
    i, j = grids()
    ref[0:HALF, 0:HALF] = cross
    ref[0:HALF, HALF:BLK] = jnp.where(i >= j, upper, lower)
    ref[HALF:TALL, 0:HALF] = jnp.broadcast_to(
        jnp.sum(jnp.where(i == j, lower, 0.0), axis=0, keepdims=True), (SUB, HALF)
    )
    ref[HALF:TALL, HALF:BLK] = jnp.zeros((SUB, HALF), f32)


def unpacked(value):
    i, j = grids()
    cross, mixed, diagonal = value[0:HALF, 0:HALF], value[0:HALF, HALF:BLK], value[HALF : HALF + 1, 0:HALF]
    turned = mixed.T
    upper = jnp.where(i >= j, mixed, turned)
    lower = jnp.where(i < j, mixed, jnp.where(i > j, turned, diagonal))
    return upper, cross, lower


def gram_kernel(here_ref, acts_ref, out_ref, *, other):
    c = here_ref[2]
    first = (1 - c if other else c) * PER_CORE
    for k in range(PER_CORE):
        start = pl.multiple_of((first + k) * BLK, BLK)
        part = acts_ref[:, pl.ds(start, BLK)]
        total = lax.dot_general(part, part, (((0,), (0,)), ((), ())), preferred_element_type=f32)
        store_packed(
            out_ref.at[k], total[0:HALF, 0:HALF], total[HALF:BLK, 0:HALF], total[HALF:BLK, HALF:BLK]
        )


def parts_kernel(here_ref, mine_ref, got_ref, pair_ref, *out_refs):
    c, own = here_ref[2], own_slot(here_ref)
    single = [offset for offset in OFFSETS if offset not in PAIR]
    targets = [(offset, pair_ref.at[n]) for n, offset in enumerate(PAIR)] + list(zip(single, out_refs))
    for offset, out_ref in targets:
        slot = (own + N_Z + offset) % N_Z
        k = rank(slot, c)

        @pl.when(holds(slot, c))
        def _():
            out_ref[...] = mine_ref[k] + got_ref[k]


def small_inverse(d):
    d = dict(d)

    def at(i, j):
        return d[(i, j)] if i >= j else d[(j, i)]

    for k in range(SUB):
        inv = 1.0 / at(k, k)
        b = {i: at(i, k) * inv for i in range(SUB) if i != k}
        for i in b:
            for j in b:
                if j <= i:
                    d[(i, j)] = d[(i, j)] - b[i] * at(j, k)
        for i in b:
            d[(max(i, k), min(i, k))] = b[i]
        d[(k, k)] = -inv
    return d


def summed(terms):
    while len(terms) > 1:
        terms = [terms[n] + terms[n + 1] for n in range(0, len(terms), 2)]
    return terms[0]


def dot(a, b, dims=((1,), (0,))):
    return lax.dot_general(
        a, b, (dims, ((), ())), precision=lax.Precision.HIGHEST, preferred_element_type=f32
    )


def half_inverse(value, rows_ref):
    count = HALF // SUB
    tiles = [value[SUB * v : SUB * v + SUB] for v in range(count)]
    lane = lax.broadcasted_iota(jnp.int32, (SUB, HALF), 1)
    line = lax.broadcasted_iota(jnp.int32, (SUB, HALF), 0)
    lower, scaled = [], []

    def spread(v):
        return jnp.broadcast_to(v, (SUB, HALF))

    for t, pivot in enumerate(tiles):
        first = SUB * t
        inside = (lane >= first) & (lane < first + SUB)
        rows_ref[first : first + SUB, :] = pivot
        each = [rows_ref[pl.ds(first + j, SUB, stride=0), :] for j in range(SUB)]
        minus = small_inverse(
            {
                (i, j): spread(each[i][:, first + j : first + j + 1])
                for i in range(SUB)
                for j in range(i + 1)
            }
        )
        rows = [
            jnp.where(lane == first + j, 1.0, jnp.where(inside, 0.0, each[j])) for j in range(SUB)
        ]
        new = [
            summed([minus[(max(i, j), min(i, j))] * rows[j] for j in range(SUB)])
            for i in range(SUB)
        ]
        own = jnp.zeros((SUB, HALF), f32)
        for j in range(SUB):
            own = jnp.where(line == j, -new[j], own)
        scaled.append(jnp.where(lane < first + SUB, own, 0.0))
        lower.append(jnp.where(lane < first, pivot, jnp.where(lane == line + first, 1.0, 0.0)))
        for v in range(t + 1, count):
            update = summed(
                [spread(tiles[v][:, first + j : first + j + 1]) * new[j] for j in range(SUB)]
            )
            tiles[v] = jnp.where(inside, 0.0, tiles[v]) + update
    return dot(jnp.concatenate(lower, axis=0), jnp.concatenate(scaled, axis=0), ((0,), (0,)))


def invert_kernel(here_ref, a_ref, b_ref, out_ref, rows_ref, *, all_tokens):
    @pl.when(holds(own_slot(here_ref), here_ref[2]))
    def _():
        upper, cross, lower = unpacked((a_ref[...] + b_ref[...]) * (1.0 / all_tokens))
        i, j = grids()
        same = i == j
        trace = jnp.sum(
            jnp.sum(jnp.where(same, upper + lower, 0.0), axis=0, keepdims=True), axis=1, keepdims=True
        )
        damping = damping_ratio * trace / BLK
        shift = jnp.where(same, damping, 0.0)
        first = half_inverse(upper + shift, rows_ref.at[0])
        w = dot(cross, first)
        second = half_inverse(lower + shift - dot(w, cross, ((1,), (1,))), rows_ref.at[1])
        x = dot(second, w)
        store_packed(out_ref, first + dot(w, x, ((0,), (0,))), -x, second)


def unpack_kernel(here_ref, *refs):
    in_refs, (full_ref, mine_ref, theirs_ref, block_ref, done) = refs[:N_Z], refs[N_Z:]
    c, own = here_ref[2], own_slot(here_ref)
    start = (here_ref[0] * N_Z + here_ref[1]) * 2

    def rows(k, core):
        return block_ref[k, pl.ds(pl.multiple_of((start + core) * SUB, SUB), SUB), :]

    def leave(k):
        return pltpu.make_async_copy(block_ref.at[k], full_ref.at[k], done.at[k])

    for offset, ref in zip(OFFSETS, in_refs):
        slot = (own + N_Z + offset) % N_Z
        k = rank(slot, c)

        @pl.when(holds(slot, c))
        def _():
            upper, cross, lower = unpacked(ref[...])
            block_ref[k, 0:HALF, 0:HALF] = upper
            block_ref[k, 0:HALF, HALF:BLK] = cross.T
            block_ref[k, HALF:BLK, 0:HALF] = cross
            block_ref[k, HALF:BLK, HALF:BLK] = lower
            leave(k).start()
            mine_ref[k] = rows(k, c)
            theirs_ref[k] = rows(k, 1 - c)

    for k in range(PER_CORE):
        leave(k).wait()


def precond_kernel(here_ref, owner_ref, own_ref, other_ref, grad_ref, out_ref, table_ref):
    step = pl.program_id(0)
    k = step % PER_CORE

    @pl.when(step < PER_CORE)
    def _():
        out_ref[...] = dot(own_ref[k], grad_ref[...])

    @pl.when(step >= PER_CORE)
    def _():
        out_ref[...] = dot(other_ref[k], grad_ref[...])

    @pl.when(step == 0)
    def _():
        sections, nblocks = owner_ref.shape
        for j in range(HOST):
            table_ref[j] = -1

        def section(s, count):
            for b in range(nblocks):
                hit = owner_ref[s, b] == here_ref[3]

                @pl.when(hit)
                def _(count=count):
                    table_ref[count] = s * nblocks + (b + here_ref[2] * PER_CORE) % nblocks

                count = count + hit.astype(jnp.int32)
            return count

        lax.fori_loop(0, sections, section, jnp.int32(0))


def hosted_kernel(table_ref, rows_ref, out_ref):
    nblocks = rows_ref.shape[1]
    for j in range(HOST):
        source = table_ref[j]
        at = jnp.maximum(source, 0)
        rows = rows_ref[at // nblocks, at % nblocks]
        out_ref[j] = jnp.where(source >= 0, rows, 0.0)


def call(kernel, out_shape, n_smem, n_vmem, scratch=()):
    out_specs = jax.tree.map(lambda _: pl.BlockSpec(memory_space=VMEM), out_shape)
    return pl.pallas_call(
        kernel,
        out_shape=out_shape,
        in_specs=[pl.BlockSpec(memory_space=pltpu.SMEM)] * n_smem
        + [pl.BlockSpec(memory_space=VMEM)] * n_vmem,
        out_specs=out_specs,
        scratch_shapes=scratch,
        compiler_params=pltpu.CompilerParams(vmem_limit_bytes=LIMIT),
    )


def shape(*dims):
    return jax.ShapeDtypeStruct(dims, f32)


IN_VMEM = pl.BlockSpec(memory_space=VMEM)
IN_SMEM = pl.BlockSpec(memory_space=pltpu.SMEM)


def unpack(here, values):
    return pl.pallas_call(
        unpack_kernel,
        out_shape=[shape(PER_CORE, BLK, BLK)] + [shape(PER_CORE, SUB, BLK)] * 2,
        in_specs=[IN_SMEM] + [IN_VMEM] * N_Z,
        out_specs=[pl.BlockSpec(memory_space=pltpu.HBM), IN_VMEM, IN_VMEM],
        scratch_shapes=[VMEM((PER_CORE, BLK, BLK), f32), pltpu.SemaphoreType.DMA((PER_CORE,))],
        compiler_params=pltpu.CompilerParams(vmem_limit_bytes=LIMIT),
    )(here, *values)


def preconditioned(here, owner_of, own, other, grad):
    rows, columns = grad.shape

    def block(i, here_ref):
        c = here_ref[2]
        return jnp.where(i < PER_CORE, c * PER_CORE + i, (1 - c) * PER_CORE + i - PER_CORE), 0

    part = pl.BlockSpec((BLK, columns), block)
    return pl.pallas_call(
        precond_kernel,
        grid_spec=pltpu.PrefetchScalarGridSpec(
            num_scalar_prefetch=1,
            grid=(rows // BLK,),
            in_specs=[IN_SMEM, IN_VMEM, IN_VMEM, part],
            out_specs=[part, IN_SMEM],
        ),
        out_shape=[shape(rows, columns), jax.ShapeDtypeStruct((HOST,), jnp.int32)],
        cost_estimate=pl.CostEstimate(
            flops=12 * rows * BLK * columns, bytes_accessed=16 * rows * columns, transcendentals=0
        ),
        compiler_params=pltpu.CompilerParams(vmem_limit_bytes=LIMIT),
    )(here, owner_of, own, other, grad)


def shards(acts, grad, owner_of):
    section_count = lax.axis_size("pipe")
    all_tokens = acts.shape[1] * lax.axis_size(DP)
    here = jnp.stack([lax.axis_index(a) for a in ("x", "z", "c", "pipe")]).astype(jnp.int32)
    features = acts[0]
    one = shape(TALL, BLK)
    packed = shape(PER_CORE, TALL, BLK)
    got = across_cores(call(functools.partial(gram_kernel, other=True), packed, 1, 1)(here, features))
    mine = call(functools.partial(gram_kernel, other=False), packed, 1, 1)(here, features)
    single = [offset for offset in OFFSETS if offset not in PAIR]
    parts = call(parts_kernel, [shape(2, TALL, BLK)] + [one] * len(single), 1, 2)(here, mine, got)
    part = dict(zip(single, parts[1:]))

    pair = across_x(parts[0])
    far = [along_z(part[2], 2), along_z(part[-2], -2)]
    across = across_x(part[4])
    near = [along_z(part[1] + pair[0], 1), along_z(part[-1] + pair[1], -1)]
    half = part[0] + across + far[0] + far[1] + near[0] + near[1]
    other_half = to_twin(half)
    invert = functools.partial(invert_kernel, all_tokens=all_tokens)
    inverse = call(invert, one, 1, 2, [VMEM((2, HALF, HALF), f32)])(here, half, other_half)

    held = {0: inverse, -1: along_z(inverse, 1), 1: along_z(inverse, -1)}
    held[4] = across_x(inverse)
    held[-2], held[2] = along_z(inverse, 2), along_z(inverse, -2)
    held[3], held[5] = across_x(held[-1]), across_x(held[1])
    own, own_rows, their_rows = unpack(here, [held[k] for k in OFFSETS])
    other_rows = across_cores(their_rows)
    rows = jnp.concatenate([own_rows, other_rows])
    sent = jnp.broadcast_to(rows[None], (section_count, *rows.shape))
    own, sent = lax.optimization_barrier((own, sent))
    other = across_cores(own)
    everyone = lax.all_to_all(sent, "pipe", 0, 0, tiled=True)
    precond, table = preconditioned(here, owner_of, own, other, grad)
    hosted = call(hosted_kernel, shape(HOST, SUB, BLK), 1, 1)(table, everyone)
    return (precond, hosted[None])


def solution(mesh):
    torus = Mesh(mesh.devices.reshape(mesh.shape["pipe"], 2, N_Z, 2), ("pipe", "x", "z", "c"))
    placed = (P("pipe", DP, None), P("pipe", DP), P())
    return jax.shard_map(
        shards,
        mesh=torus,
        in_specs=placed,
        out_specs=(P("pipe", DP), P("pipe", None, DP, None)),
        check_vma=False,
    )
```

```python
import functools

import jax
import jax.numpy as jnp
from jax import lax
from jax.experimental import pallas as pl
from jax.experimental.pallas import tpu as pltpu
from jax.sharding import Mesh
from jax.sharding import PartitionSpec as P

BLK = 256
HALF = BLK // 2
SUB = 8
NB = 12
PER_CORE = NB // 2
HOST = 24
TALL = HALF + SUB
N_Z = 8
DP = ("x", "z", "c")
damping_ratio = 0.1
LIMIT = 8 * 1024 * 1024
VMEM = pltpu.VMEM
f32 = jnp.float32


def own_slot(here_ref):
    x, z, c = here_ref[0], here_ref[1], here_ref[2]
    return (z + N_Z - 2 * (1 - 2 * c) * x) % N_Z


def slot_at(here_ref, offset):
    way = jnp.where(here_ref[0] == here_ref[2], 1, -1)
    return (own_slot(here_ref) + N_Z + way * offset) % N_Z


def holds(slot, c):
    return (slot % 4) != jnp.where(c == 0, 3, 1)


def rank(slot, c):
    return (slot // 4) * 3 + jnp.where(c == 0, slot % 4, (slot % 4 + 1) // 2)


OFFSETS = (0, 1, -1, 2, -2, 3, -3, -4)
PAIR = (-3, -4)


def number(x, z, c):
    return (x * N_Z + z % N_Z) * 2 + c


PLACES = [(x, z, c) for x in range(2) for z in range(N_Z) for c in range(2)]


def along_z(value, step):
    pairs = [
        (number(x, z, c), number(x, z + (step if x == c else -step), c)) for x, z, c in PLACES
    ]
    return lax.ppermute(value, DP, pairs)


def across_x(value):
    return lax.ppermute(value, "x", [(0, 1), (1, 0)])


def to_twin(value):
    pairs = [
        (number(x, z, c), number(1 - x, z + (2 if x == c else -2), c)) for x, z, c in PLACES
    ]
    return lax.ppermute(value, DP, pairs)


def across_cores(value):
    return lax.ppermute(value, "c", [(0, 1), (1, 0)])


def grids():
    return (
        lax.broadcasted_iota(jnp.int32, (HALF, HALF), 0),
        lax.broadcasted_iota(jnp.int32, (HALF, HALF), 1),
    )


def store_packed(ref, upper, cross, lower):
    i, j = grids()
    ref[0:HALF, 0:HALF] = cross
    ref[0:HALF, HALF:BLK] = jnp.where(i >= j, upper, lower)
    ref[HALF:TALL, 0:HALF] = jnp.broadcast_to(
        jnp.sum(jnp.where(i == j, lower, 0.0), axis=0, keepdims=True), (SUB, HALF)
    )
    ref[HALF:TALL, HALF:BLK] = jnp.zeros((SUB, HALF), f32)


def unpacked(value):
    i, j = grids()
    cross, mixed, diagonal = value[0:HALF, 0:HALF], value[0:HALF, HALF:BLK], value[HALF : HALF + 1, 0:HALF]
    turned = mixed.T
    upper = jnp.where(i >= j, mixed, turned)
    lower = jnp.where(i < j, mixed, jnp.where(i > j, turned, diagonal))
    return upper, cross, lower


def gram_kernel(here_ref, acts_ref, out_ref, *, other):
    c = here_ref[2]
    first = (1 - c if other else c) * PER_CORE
    for k in range(PER_CORE):
        start = pl.multiple_of((first + k) * BLK, BLK)
        part = acts_ref[:, pl.ds(start, BLK)]
        total = lax.dot_general(part, part, (((0,), (0,)), ((), ())), preferred_element_type=f32)
        store_packed(
            out_ref.at[k], total[0:HALF, 0:HALF], total[HALF:BLK, 0:HALF], total[HALF:BLK, HALF:BLK]
        )


def parts_kernel(here_ref, mine_ref, got_ref, pair_ref, *out_refs):
    c = here_ref[2]
    single = [offset for offset in OFFSETS if offset not in PAIR]
    targets = [(offset, pair_ref.at[n]) for n, offset in enumerate(PAIR)] + list(zip(single, out_refs))
    for offset, out_ref in targets:
        slot = slot_at(here_ref, offset)
        k = rank(slot, c)

        @pl.when(holds(slot, c))
        def _():
            out_ref[...] = mine_ref[k] + got_ref[k]


def small_inverse(d):
    d = dict(d)

    def at(i, j):
        return d[(i, j)] if i >= j else d[(j, i)]

    for k in range(SUB):
        inv = 1.0 / at(k, k)
        b = {i: at(i, k) * inv for i in range(SUB) if i != k}
        for i in b:
            for j in b:
                if j <= i:
                    d[(i, j)] = d[(i, j)] - b[i] * at(j, k)
        for i in b:
            d[(max(i, k), min(i, k))] = b[i]
        d[(k, k)] = -inv
    return d


def summed(terms):
    while len(terms) > 1:
        terms = [terms[n] + terms[n + 1] for n in range(0, len(terms), 2)]
    return terms[0]


def dot(a, b, dims=((1,), (0,))):
    return lax.dot_general(
        a, b, (dims, ((), ())), precision=lax.Precision.HIGHEST, preferred_element_type=f32
    )


def half_inverse(value, rows_ref):
    count = HALF // SUB
    tiles = [value[SUB * v : SUB * v + SUB] for v in range(count)]
    lane = lax.broadcasted_iota(jnp.int32, (SUB, HALF), 1)
    line = lax.broadcasted_iota(jnp.int32, (SUB, HALF), 0)
    lower, scaled = [], []

    def spread(v):
        return jnp.broadcast_to(v, (SUB, HALF))

    for t, pivot in enumerate(tiles):
        first = SUB * t
        inside = (lane >= first) & (lane < first + SUB)
        rows_ref[first : first + SUB, :] = pivot
        each = [rows_ref[pl.ds(first + j, SUB, stride=0), :] for j in range(SUB)]
        minus = small_inverse(
            {
                (i, j): spread(each[i][:, first + j : first + j + 1])
                for i in range(SUB)
                for j in range(i + 1)
            }
        )
        rows = [
            jnp.where(lane == first + j, 1.0, jnp.where(inside, 0.0, each[j])) for j in range(SUB)
        ]
        new = [
            summed([minus[(max(i, j), min(i, j))] * rows[j] for j in range(SUB)])
            for i in range(SUB)
        ]
        own = jnp.zeros((SUB, HALF), f32)
        for j in range(SUB):
            own = jnp.where(line == j, -new[j], own)
        scaled.append(jnp.where(lane < first + SUB, own, 0.0))
        lower.append(jnp.where(lane < first, pivot, jnp.where(lane == line + first, 1.0, 0.0)))
        for v in range(t + 1, count):
            update = summed(
                [spread(tiles[v][:, first + j : first + j + 1]) * new[j] for j in range(SUB)]
            )
            tiles[v] = jnp.where(inside, 0.0, tiles[v]) + update
    return dot(jnp.concatenate(lower, axis=0), jnp.concatenate(scaled, axis=0), ((0,), (0,)))


def invert_kernel(here_ref, a_ref, b_ref, out_ref, rows_ref, *, all_tokens):
    @pl.when(holds(own_slot(here_ref), here_ref[2]))
    def _():
        upper, cross, lower = unpacked((a_ref[...] + b_ref[...]) * (1.0 / all_tokens))
        i, j = grids()
        same = i == j
        trace = jnp.sum(
            jnp.sum(jnp.where(same, upper + lower, 0.0), axis=0, keepdims=True), axis=1, keepdims=True
        )
        damping = damping_ratio * trace / BLK
        shift = jnp.where(same, damping, 0.0)
        first = half_inverse(upper + shift, rows_ref.at[0])
        w = dot(cross, first)
        second = half_inverse(lower + shift - dot(w, cross, ((1,), (1,))), rows_ref.at[1])
        x = dot(second, w)
        store_packed(out_ref, first + dot(w, x, ((0,), (0,))), -x, second)


def unpack_kernel(here_ref, *refs):
    in_refs, (full_ref, mine_ref, theirs_ref, block_ref, done) = refs[:N_Z], refs[N_Z:]
    c = here_ref[2]
    start = (here_ref[0] * N_Z + here_ref[1]) * 2

    def rows(k, core):
        return block_ref[k, pl.ds(pl.multiple_of((start + core) * SUB, SUB), SUB), :]

    def leave(k):
        return pltpu.make_async_copy(block_ref.at[k], full_ref.at[k], done.at[k])

    for offset, ref in zip(OFFSETS, in_refs):
        slot = slot_at(here_ref, offset)
        k = rank(slot, c)

        @pl.when(holds(slot, c))
        def _():
            upper, cross, lower = unpacked(ref[...])
            block_ref[k, 0:HALF, 0:HALF] = upper
            block_ref[k, 0:HALF, HALF:BLK] = cross.T
            block_ref[k, HALF:BLK, 0:HALF] = cross
            block_ref[k, HALF:BLK, HALF:BLK] = lower
            leave(k).start()
            mine_ref[k] = rows(k, c)
            theirs_ref[k] = rows(k, 1 - c)

    for k in range(PER_CORE):
        leave(k).wait()


def precond_kernel(here_ref, owner_ref, own_ref, other_ref, grad_ref, out_ref, table_ref):
    step = pl.program_id(0)
    k = step % PER_CORE

    @pl.when(step < PER_CORE)
    def _():
        out_ref[...] = dot(own_ref[k], grad_ref[...])

    @pl.when(step >= PER_CORE)
    def _():
        out_ref[...] = dot(other_ref[k], grad_ref[...])

    @pl.when(step == 0)
    def _():
        sections, nblocks = owner_ref.shape
        for j in range(HOST):
            table_ref[j] = -1

        def section(s, count):
            for b in range(nblocks):
                hit = owner_ref[s, b] == here_ref[3]

                @pl.when(hit)
                def _(count=count):
                    table_ref[count] = s * nblocks + (b + here_ref[2] * PER_CORE) % nblocks

                count = count + hit.astype(jnp.int32)
            return count

        lax.fori_loop(0, sections, section, jnp.int32(0))


def hosted_kernel(table_ref, rows_ref, out_ref):
    nblocks = rows_ref.shape[1]
    for j in range(HOST):
        source = table_ref[j]
        at = jnp.maximum(source, 0)
        rows = rows_ref[at // nblocks, at % nblocks]
        out_ref[j] = jnp.where(source >= 0, rows, 0.0)


def call(kernel, out_shape, n_smem, n_vmem, scratch=()):
    out_specs = jax.tree.map(lambda _: pl.BlockSpec(memory_space=VMEM), out_shape)
    return pl.pallas_call(
        kernel,
        out_shape=out_shape,
        in_specs=[pl.BlockSpec(memory_space=pltpu.SMEM)] * n_smem
        + [pl.BlockSpec(memory_space=VMEM)] * n_vmem,
        out_specs=out_specs,
        scratch_shapes=scratch,
        compiler_params=pltpu.CompilerParams(vmem_limit_bytes=LIMIT),
    )


def shape(*dims):
    return jax.ShapeDtypeStruct(dims, f32)


IN_VMEM = pl.BlockSpec(memory_space=VMEM)
IN_SMEM = pl.BlockSpec(memory_space=pltpu.SMEM)


def unpack(here, values):
    return pl.pallas_call(
        unpack_kernel,
        out_shape=[shape(PER_CORE, BLK, BLK)] + [shape(PER_CORE, SUB, BLK)] * 2,
        in_specs=[IN_SMEM] + [IN_VMEM] * N_Z,
        out_specs=[pl.BlockSpec(memory_space=pltpu.HBM), IN_VMEM, IN_VMEM],
        scratch_shapes=[VMEM((PER_CORE, BLK, BLK), f32), pltpu.SemaphoreType.DMA((PER_CORE,))],
        compiler_params=pltpu.CompilerParams(vmem_limit_bytes=LIMIT),
    )(here, *values)


def preconditioned(here, owner_of, own, other, grad):
    rows, columns = grad.shape

    def block(i, here_ref):
        c = here_ref[2]
        return jnp.where(i < PER_CORE, c * PER_CORE + i, (1 - c) * PER_CORE + i - PER_CORE), 0

    part = pl.BlockSpec((BLK, columns), block)
    return pl.pallas_call(
        precond_kernel,
        grid_spec=pltpu.PrefetchScalarGridSpec(
            num_scalar_prefetch=1,
            grid=(rows // BLK,),
            in_specs=[IN_SMEM, IN_VMEM, IN_VMEM, part],
            out_specs=[part, IN_SMEM],
        ),
        out_shape=[shape(rows, columns), jax.ShapeDtypeStruct((HOST,), jnp.int32)],
        cost_estimate=pl.CostEstimate(
            flops=12 * rows * BLK * columns, bytes_accessed=16 * rows * columns, transcendentals=0
        ),
        compiler_params=pltpu.CompilerParams(vmem_limit_bytes=LIMIT),
    )(here, owner_of, own, other, grad)


def shards(acts, grad, owner_of):
    section_count = lax.axis_size("pipe")
    all_tokens = acts.shape[1] * lax.axis_size(DP)
    here = jnp.stack([lax.axis_index(a) for a in ("x", "z", "c", "pipe")]).astype(jnp.int32)
    features = acts[0]
    one = shape(TALL, BLK)
    packed = shape(PER_CORE, TALL, BLK)
    got = across_cores(call(functools.partial(gram_kernel, other=True), packed, 1, 1)(here, features))
    mine = call(functools.partial(gram_kernel, other=False), packed, 1, 1)(here, features)
    single = [offset for offset in OFFSETS if offset not in PAIR]
    parts = call(parts_kernel, [shape(2, TALL, BLK)] + [one] * len(single), 1, 2)(here, mine, got)
    part = dict(zip(single, parts[1:]))

    pair = across_x(parts[0])
    far = [along_z(part[offset], offset) for offset in (3, -2, -1)]
    near = [along_z(part[1] + pair[0], 1), along_z(part[2] + pair[1], 2)]
    half = part[0] + far[0] + far[1] + far[2] + near[0] + near[1]
    other_half = to_twin(half)
    invert = functools.partial(invert_kernel, all_tokens=all_tokens)
    inverse = call(invert, one, 1, 2, [VMEM((2, HALF, HALF), f32)])(here, half, other_half)

    held = {0: inverse}
    for offset in (1, 2, 3, -2, -1):
        held[offset] = along_z(inverse, -offset)
    held[-3], held[-4] = across_x(held[1]), across_x(held[2])
    own, own_rows, their_rows = unpack(here, [held[k] for k in OFFSETS])
    other_rows = across_cores(their_rows)
    rows = jnp.concatenate([own_rows, other_rows])
    sent = jnp.broadcast_to(rows[None], (section_count, *rows.shape))
    own, sent, grad = lax.optimization_barrier((own, sent, grad))
    other = across_cores(own)
    everyone = lax.all_to_all(sent, "pipe", 0, 0, tiled=True)
    precond, table = preconditioned(here, owner_of, own, other, grad)
    hosted = call(hosted_kernel, shape(HOST, SUB, BLK), 1, 1)(table, everyone)
    return (precond, hosted[None])


def solution(mesh):
    torus = Mesh(mesh.devices.reshape(mesh.shape["pipe"], 2, N_Z, 2), ("pipe", "x", "z", "c"))
    placed = (P("pipe", DP, None), P("pipe", DP), P())
    return jax.shard_map(
        shards,
        mesh=torus,
        in_specs=placed,
        out_specs=(P("pipe", DP), P("pipe", None, DP, None)),
        check_vma=False,
    )
```

```python
import functools

import jax
import jax.numpy as jnp
from jax import lax
from jax.experimental import pallas as pl
from jax.experimental.pallas import tpu as pltpu
from jax.sharding import Mesh
from jax.sharding import PartitionSpec as P

BLK = 256
HALF = BLK // 2
SUB = 8
NB = 12
PER_CORE = NB // 2
HOST = 24
TALL = HALF + SUB
N_Z = 8
DP = ("x", "z", "c")
damping_ratio = 0.1
LIMIT = 8 * 1024 * 1024
VMEM = pltpu.VMEM
f32 = jnp.float32


def own_slot(here_ref):
    x, z, c = here_ref[0], here_ref[1], here_ref[2]
    return (z + N_Z - 2 * (1 - 2 * c) * x) % N_Z


def slot_at(here_ref, offset):
    way = jnp.where(here_ref[0] == here_ref[2], 1, -1)
    return (own_slot(here_ref) + N_Z + way * offset) % N_Z


def holds(slot, c):
    return (slot % 4) != jnp.where(c == 0, 3, 1)


def rank(slot, c):
    return (slot // 4) * 3 + jnp.where(c == 0, slot % 4, (slot % 4 + 1) // 2)


OFFSETS = (0, 1, -1, 2, -2, 3, -3, -4)
PAIR = (-3, -4)


def number(x, z, c):
    return (x * N_Z + z % N_Z) * 2 + c


PLACES = [(x, z, c) for x in range(2) for z in range(N_Z) for c in range(2)]


def along_z(value, step):
    pairs = [
        (number(x, z, c), number(x, z + (step if x == c else -step), c)) for x, z, c in PLACES
    ]
    return lax.ppermute(value, DP, pairs)


def across_x(value):
    return lax.ppermute(value, "x", [(0, 1), (1, 0)])


def to_twin(value):
    pairs = [
        (number(x, z, c), number(1 - x, z + (2 if x == c else -2), c)) for x, z, c in PLACES
    ]
    return lax.ppermute(value, DP, pairs)


def across_cores(value):
    return lax.ppermute(value, "c", [(0, 1), (1, 0)])


def grids():
    return (
        lax.broadcasted_iota(jnp.int32, (HALF, HALF), 0),
        lax.broadcasted_iota(jnp.int32, (HALF, HALF), 1),
    )


def store_packed(ref, upper, cross, lower):
    i, j = grids()
    ref[0:HALF, 0:HALF] = cross
    ref[0:HALF, HALF:BLK] = jnp.where(i >= j, upper, lower)
    ref[HALF:TALL, 0:HALF] = jnp.broadcast_to(
        jnp.sum(jnp.where(i == j, lower, 0.0), axis=0, keepdims=True), (SUB, HALF)
    )
    ref[HALF:TALL, HALF:BLK] = jnp.zeros((SUB, HALF), f32)


def unpacked(value):
    i, j = grids()
    cross, mixed, diagonal = value[0:HALF, 0:HALF], value[0:HALF, HALF:BLK], value[HALF : HALF + 1, 0:HALF]
    turned = mixed.T
    upper = jnp.where(i >= j, mixed, turned)
    lower = jnp.where(i < j, mixed, jnp.where(i > j, turned, diagonal))
    return upper, cross, lower


def gram_kernel(here_ref, acts_ref, out_ref, *, other):
    c = here_ref[2]
    first = (1 - c if other else c) * PER_CORE
    for k in range(PER_CORE):
        start = pl.multiple_of((first + k) * BLK, BLK)
        part = acts_ref[:, pl.ds(start, BLK)]
        total = lax.dot_general(part, part, (((0,), (0,)), ((), ())), preferred_element_type=f32)
        store_packed(
            out_ref.at[k], total[0:HALF, 0:HALF], total[HALF:BLK, 0:HALF], total[HALF:BLK, HALF:BLK]
        )


def parts_kernel(here_ref, mine_ref, got_ref, pair_ref, *out_refs):
    c = here_ref[2]
    single = [offset for offset in OFFSETS if offset not in PAIR]
    targets = [(offset, pair_ref.at[n]) for n, offset in enumerate(PAIR)] + list(zip(single, out_refs))
    for offset, out_ref in targets:
        slot = slot_at(here_ref, offset)
        k = rank(slot, c)

        @pl.when(holds(slot, c))
        def _():
            out_ref[...] = mine_ref[k] + got_ref[k]


def small_inverse(d):
    d = dict(d)

    def at(i, j):
        return d[(i, j)] if i >= j else d[(j, i)]

    for k in range(SUB):
        inv = 1.0 / at(k, k)
        b = {i: at(i, k) * inv for i in range(SUB) if i != k}
        for i in b:
            for j in b:
                if j <= i:
                    d[(i, j)] = d[(i, j)] - b[i] * at(j, k)
        for i in b:
            d[(max(i, k), min(i, k))] = b[i]
        d[(k, k)] = -inv
    return d


def summed(terms):
    while len(terms) > 1:
        terms = [terms[n] + terms[n + 1] for n in range(0, len(terms), 2)]
    return terms[0]


def dot(a, b, dims=((1,), (0,))):
    return lax.dot_general(
        a, b, (dims, ((), ())), precision=lax.Precision.HIGHEST, preferred_element_type=f32
    )


def half_inverse(value, rows_ref):
    count = HALF // SUB
    tiles = [value[SUB * v : SUB * v + SUB] for v in range(count)]
    lane = lax.broadcasted_iota(jnp.int32, (SUB, HALF), 1)
    line = lax.broadcasted_iota(jnp.int32, (SUB, HALF), 0)
    lower, scaled = [], []

    def spread(v):
        return jnp.broadcast_to(v, (SUB, HALF))

    for t, pivot in enumerate(tiles):
        first = SUB * t
        inside = (lane >= first) & (lane < first + SUB)
        rows_ref[first : first + SUB, :] = pivot
        each = [rows_ref[pl.ds(first + j, SUB, stride=0), :] for j in range(SUB)]
        minus = small_inverse(
            {
                (i, j): spread(each[i][:, first + j : first + j + 1])
                for i in range(SUB)
                for j in range(i + 1)
            }
        )
        rows = [
            jnp.where(lane == first + j, 1.0, jnp.where(inside, 0.0, each[j])) for j in range(SUB)
        ]
        new = [
            summed([minus[(max(i, j), min(i, j))] * rows[j] for j in range(SUB)])
            for i in range(SUB)
        ]
        own = jnp.zeros((SUB, HALF), f32)
        for j in range(SUB):
            own = jnp.where(line == j, -new[j], own)
        scaled.append(jnp.where(lane < first + SUB, own, 0.0))
        lower.append(jnp.where(lane < first, pivot, jnp.where(lane == line + first, 1.0, 0.0)))
        for v in range(t + 1, count):
            update = summed(
                [spread(tiles[v][:, first + j : first + j + 1]) * new[j] for j in range(SUB)]
            )
            tiles[v] = jnp.where(inside, 0.0, tiles[v]) + update
    return dot(jnp.concatenate(lower, axis=0), jnp.concatenate(scaled, axis=0), ((0,), (0,)))


def invert_kernel(here_ref, a_ref, b_ref, out_ref, rows_ref, *, all_tokens):
    @pl.when(holds(own_slot(here_ref), here_ref[2]))
    def _():
        upper, cross, lower = unpacked((a_ref[...] + b_ref[...]) * (1.0 / all_tokens))
        i, j = grids()
        same = i == j
        trace = jnp.sum(
            jnp.sum(jnp.where(same, upper + lower, 0.0), axis=0, keepdims=True), axis=1, keepdims=True
        )
        damping = damping_ratio * trace / BLK
        shift = jnp.where(same, damping, 0.0)
        first = half_inverse(upper + shift, rows_ref.at[0])
        w = dot(cross, first)
        second = half_inverse(lower + shift - dot(w, cross, ((1,), (1,))), rows_ref.at[1])
        x = dot(second, w)
        store_packed(out_ref, first + dot(w, x, ((0,), (0,))), -x, second)


def unpack_kernel(here_ref, *refs):
    in_refs, (full_ref, mine_ref, theirs_ref, block_ref, done) = refs[:N_Z], refs[N_Z:]
    c = here_ref[2]
    start = (here_ref[0] * N_Z + here_ref[1]) * 2

    def rows(k, core):
        return block_ref[k, pl.ds(pl.multiple_of((start + core) * SUB, SUB), SUB), :]

    def leave(k):
        return pltpu.make_async_copy(block_ref.at[k], full_ref.at[k], done.at[k])

    for offset, ref in zip(OFFSETS, in_refs):
        slot = slot_at(here_ref, offset)
        k = rank(slot, c)

        @pl.when(holds(slot, c))
        def _():
            upper, cross, lower = unpacked(ref[...])
            block_ref[k, 0:HALF, 0:HALF] = upper
            block_ref[k, 0:HALF, HALF:BLK] = cross.T
            block_ref[k, HALF:BLK, 0:HALF] = cross
            block_ref[k, HALF:BLK, HALF:BLK] = lower
            leave(k).start()
            mine_ref[k] = rows(k, c)
            theirs_ref[k] = rows(k, 1 - c)

    for k in range(PER_CORE):
        leave(k).wait()


def precond_kernel(here_ref, owner_ref, own_ref, other_ref, grad_ref, out_ref, table_ref):
    step = pl.program_id(0)
    k = step % PER_CORE

    @pl.when(step < PER_CORE)
    def _():
        out_ref[...] = dot(own_ref[k], grad_ref[...])

    @pl.when(step >= PER_CORE)
    def _():
        out_ref[...] = dot(other_ref[k], grad_ref[...])

    @pl.when(step == 0)
    def _():
        sections, nblocks = owner_ref.shape
        for j in range(HOST):
            table_ref[j] = -1

        def section(s, count):
            for b in range(nblocks):
                hit = owner_ref[s, b] == here_ref[3]

                @pl.when(hit)
                def _(count=count):
                    table_ref[count] = s * nblocks + (b + here_ref[2] * PER_CORE) % nblocks

                count = count + hit.astype(jnp.int32)
            return count

        lax.fori_loop(0, sections, section, jnp.int32(0))


def hosted_kernel(table_ref, rows_ref, out_ref):
    nblocks = rows_ref.shape[1]
    for j in range(HOST):
        source = table_ref[j]
        at = jnp.maximum(source, 0)
        rows = rows_ref[at // nblocks, at % nblocks]
        out_ref[j] = jnp.where(source >= 0, rows, 0.0)


def call(kernel, out_shape, n_smem, n_vmem, scratch=()):
    out_specs = jax.tree.map(lambda _: pl.BlockSpec(memory_space=VMEM), out_shape)
    return pl.pallas_call(
        kernel,
        out_shape=out_shape,
        in_specs=[pl.BlockSpec(memory_space=pltpu.SMEM)] * n_smem
        + [pl.BlockSpec(memory_space=VMEM)] * n_vmem,
        out_specs=out_specs,
        scratch_shapes=scratch,
        compiler_params=pltpu.CompilerParams(vmem_limit_bytes=LIMIT),
    )


def shape(*dims):
    return jax.ShapeDtypeStruct(dims, f32)


IN_VMEM = pl.BlockSpec(memory_space=VMEM)
IN_SMEM = pl.BlockSpec(memory_space=pltpu.SMEM)


def unpack(here, values):
    return pl.pallas_call(
        unpack_kernel,
        out_shape=[shape(PER_CORE, BLK, BLK)] + [shape(PER_CORE, SUB, BLK)] * 2,
        in_specs=[IN_SMEM] + [IN_VMEM] * N_Z,
        out_specs=[pl.BlockSpec(memory_space=pltpu.HBM), IN_VMEM, IN_VMEM],
        scratch_shapes=[VMEM((PER_CORE, BLK, BLK), f32), pltpu.SemaphoreType.DMA((PER_CORE,))],
        compiler_params=pltpu.CompilerParams(vmem_limit_bytes=LIMIT),
    )(here, *values)


def preconditioned(here, owner_of, own, other, grad):
    rows, columns = grad.shape

    def block(i, here_ref):
        c = here_ref[2]
        return jnp.where(i < PER_CORE, c * PER_CORE + i, (1 - c) * PER_CORE + i - PER_CORE), 0

    part = pl.BlockSpec((BLK, columns), block)
    return pl.pallas_call(
        precond_kernel,
        grid_spec=pltpu.PrefetchScalarGridSpec(
            num_scalar_prefetch=1,
            grid=(rows // BLK,),
            in_specs=[IN_SMEM, IN_VMEM, IN_VMEM, part],
            out_specs=[part, IN_SMEM],
        ),
        out_shape=[shape(rows, columns), jax.ShapeDtypeStruct((HOST,), jnp.int32)],
        cost_estimate=pl.CostEstimate(
            flops=12 * rows * BLK * columns, bytes_accessed=16 * rows * columns, transcendentals=0
        ),
        compiler_params=pltpu.CompilerParams(vmem_limit_bytes=LIMIT),
    )(here, owner_of, own, other, grad)


def shards(acts, grad, owner_of):
    section_count = lax.axis_size("pipe")
    all_tokens = acts.shape[1] * lax.axis_size(DP)
    here = jnp.stack([lax.axis_index(a) for a in ("x", "z", "c", "pipe")]).astype(jnp.int32)
    features = acts[0]
    one = shape(TALL, BLK)
    packed = shape(PER_CORE, TALL, BLK)
    got = across_cores(call(functools.partial(gram_kernel, other=True), packed, 1, 1)(here, features))
    mine = call(functools.partial(gram_kernel, other=False), packed, 1, 1)(here, features)
    single = [offset for offset in OFFSETS if offset not in PAIR]
    parts = call(parts_kernel, [shape(2, TALL, BLK)] + [one] * len(single), 1, 2)(here, mine, got)
    part = dict(zip(single, parts[1:]))

    pair = across_x(parts[0])
    step = along_z(part[3], 1)
    far = [along_z(part[-2], -2), along_z(part[-1], -1)]
    near = [along_z(part[1] + pair[0], 1), along_z(part[2] + step + pair[1], 2)]
    half = part[0] + far[0] + far[1] + near[0] + near[1]
    other_half = to_twin(half)
    invert = functools.partial(invert_kernel, all_tokens=all_tokens)
    inverse = call(invert, one, 1, 2, [VMEM((2, HALF, HALF), f32)])(here, half, other_half)

    held = {0: inverse}
    for offset in (2, 1, -2, -1):
        held[offset] = along_z(inverse, -offset)
    held[3] = along_z(held[2], -1)
    held[-3], held[-4] = across_x(held[1]), across_x(held[2])
    own, own_rows, their_rows = unpack(here, [held[k] for k in OFFSETS])
    other_rows = across_cores(their_rows)
    rows = jnp.concatenate([own_rows, other_rows])
    sent = jnp.broadcast_to(rows[None], (section_count, *rows.shape))
    own, sent, grad = lax.optimization_barrier((own, sent, grad))
    other = across_cores(own)
    everyone = lax.all_to_all(sent, "pipe", 0, 0, tiled=True)
    precond, table = preconditioned(here, owner_of, own, other, grad)
    hosted = call(hosted_kernel, shape(HOST, SUB, BLK), 1, 1)(table, everyone)
    return (precond, hosted[None])


def solution(mesh):
    torus = Mesh(mesh.devices.reshape(mesh.shape["pipe"], 2, N_Z, 2), ("pipe", "x", "z", "c"))
    placed = (P("pipe", DP, None), P("pipe", DP), P())
    return jax.shard_map(
        shards,
        mesh=torus,
        in_specs=placed,
        out_specs=(P("pipe", DP), P("pipe", None, DP, None)),
        check_vma=False,
    )
```

```python
import functools

import jax
import jax.numpy as jnp
from jax import lax
from jax.experimental import pallas as pl
from jax.experimental.pallas import tpu as pltpu
from jax.sharding import Mesh
from jax.sharding import PartitionSpec as P

BLK = 256
HALF = BLK // 2
SUB = 8
NB = 12
PER_CORE = NB // 2
HOST = 24
TALL = 2 * HALF + SUB
N_Z = 8
DP = ("x", "z", "c")
damping_ratio = 0.1
LIMIT = 8 * 1024 * 1024
VMEM = pltpu.VMEM
f32 = jnp.float32


def own_slot(here_ref):
    return (here_ref[1] + 4 * here_ref[0]) % N_Z


def holds(slot, c):
    return (slot % 4) != jnp.where(c == 0, 3, 1)


def rank(slot, c):
    return (slot // 4) * 3 + jnp.where(c == 0, slot % 4, (slot % 4 + 1) // 2)


OFFSETS = (0, 1, -1, 2, -2, 3, 4, 5)
PAIR = (5, 3)


def along_z(value, step):
    return lax.ppermute(value, "z", [(z, (z + step) % N_Z) for z in range(N_Z)])


def across_x(value):
    return lax.ppermute(value, "x", [(0, 1), (1, 0)])


def to_twin(value):
    pairs = [(x * N_Z + z, (1 - x) * N_Z + (z + 4) % N_Z) for x in range(2) for z in range(N_Z)]
    return lax.ppermute(value, ("x", "z"), pairs)


def across_cores(value):
    return lax.ppermute(value, "c", [(0, 1), (1, 0)])


def grids():
    return (
        lax.broadcasted_iota(jnp.int32, (HALF, HALF), 0),
        lax.broadcasted_iota(jnp.int32, (HALF, HALF), 1),
    )


def store_packed(ref, upper, cross, lower):
    i, j = grids()
    ref[0:HALF, :] = cross
    ref[HALF:BLK, :] = jnp.where(i >= j, upper, lower)
    ref[BLK:TALL, :] = jnp.broadcast_to(
        jnp.sum(jnp.where(i == j, lower, 0.0), axis=0, keepdims=True), (SUB, HALF)
    )


def unpacked(value):
    i, j = grids()
    cross, mixed, diagonal = value[0:HALF], value[HALF:BLK], value[BLK : BLK + 1]
    turned = mixed.T
    upper = jnp.where(i >= j, mixed, turned)
    lower = jnp.where(i < j, mixed, jnp.where(i > j, turned, diagonal))
    return upper, cross, lower


def gram_kernel(here_ref, acts_ref, out_ref, *, other):
    c = here_ref[2]
    first = (1 - c if other else c) * PER_CORE
    for k in range(PER_CORE):
        start = pl.multiple_of((first + k) * BLK, BLK)
        part = acts_ref[:, pl.ds(start, BLK)]
        total = lax.dot_general(part, part, (((0,), (0,)), ((), ())), preferred_element_type=f32)
        store_packed(
            out_ref.at[k], total[0:HALF, 0:HALF], total[HALF:BLK, 0:HALF], total[HALF:BLK, HALF:BLK]
        )


def parts_kernel(here_ref, mine_ref, got_ref, pair_ref, *out_refs):
    c, own = here_ref[2], own_slot(here_ref)
    single = [offset for offset in OFFSETS if offset not in PAIR]
    targets = [(offset, pair_ref.at[n]) for n, offset in enumerate(PAIR)] + list(zip(single, out_refs))
    for offset, out_ref in targets:
        slot = (own + N_Z + offset) % N_Z
        k = rank(slot, c)

        @pl.when(holds(slot, c))
        def _():
            out_ref[...] = mine_ref[k] + got_ref[k]


def small_inverse(d):
    d = dict(d)

    def at(i, j):
        return d[(i, j)] if i >= j else d[(j, i)]

    for k in range(SUB):
        inv = 1.0 / at(k, k)
        b = {i: at(i, k) * inv for i in range(SUB) if i != k}
        for i in b:
            for j in b:
                if j <= i:
                    d[(i, j)] = d[(i, j)] - b[i] * at(j, k)
        for i in b:
            d[(max(i, k), min(i, k))] = b[i]
        d[(k, k)] = -inv
    return d


def summed(terms):
    while len(terms) > 1:
        terms = [terms[n] + terms[n + 1] for n in range(0, len(terms), 2)]
    return terms[0]


def dot(a, b, dims=((1,), (0,))):
    return lax.dot_general(
        a, b, (dims, ((), ())), precision=lax.Precision.HIGHEST, preferred_element_type=f32
    )


def half_inverse(value, rows_ref):
    count = HALF // SUB
    tiles = [value[SUB * v : SUB * v + SUB] for v in range(count)]
    lane = lax.broadcasted_iota(jnp.int32, (SUB, HALF), 1)
    line = lax.broadcasted_iota(jnp.int32, (SUB, HALF), 0)
    lower, scaled = [], []

    def spread(v):
        return jnp.broadcast_to(v, (SUB, HALF))

    for t, pivot in enumerate(tiles):
        first = SUB * t
        inside = (lane >= first) & (lane < first + SUB)
        rows_ref[first : first + SUB, :] = pivot
        each = [rows_ref[pl.ds(first + j, SUB, stride=0), :] for j in range(SUB)]
        minus = small_inverse(
            {
                (i, j): spread(each[i][:, first + j : first + j + 1])
                for i in range(SUB)
                for j in range(i + 1)
            }
        )
        rows = [
            jnp.where(lane == first + j, 1.0, jnp.where(inside, 0.0, each[j])) for j in range(SUB)
        ]
        new = [
            summed([minus[(max(i, j), min(i, j))] * rows[j] for j in range(SUB)])
            for i in range(SUB)
        ]
        own = jnp.zeros((SUB, HALF), f32)
        for j in range(SUB):
            own = jnp.where(line == j, -new[j], own)
        scaled.append(jnp.where(lane < first + SUB, own, 0.0))
        lower.append(jnp.where(lane < first, pivot, jnp.where(lane == line + first, 1.0, 0.0)))
        for v in range(t + 1, count):
            update = summed(
                [spread(tiles[v][:, first + j : first + j + 1]) * new[j] for j in range(SUB)]
            )
            tiles[v] = jnp.where(inside, 0.0, tiles[v]) + update
    return dot(jnp.concatenate(lower, axis=0), jnp.concatenate(scaled, axis=0), ((0,), (0,)))


def invert_kernel(here_ref, a_ref, b_ref, out_ref, rows_ref, *, all_tokens):
    @pl.when(holds(own_slot(here_ref), here_ref[2]))
    def _():
        upper, cross, lower = unpacked((a_ref[...] + b_ref[...]) * (1.0 / all_tokens))
        i, j = grids()
        same = i == j
        trace = jnp.sum(
            jnp.sum(jnp.where(same, upper + lower, 0.0), axis=0, keepdims=True), axis=1, keepdims=True
        )
        damping = damping_ratio * trace / BLK
        shift = jnp.where(same, damping, 0.0)
        first = half_inverse(upper + shift, rows_ref.at[0])
        w = dot(cross, first)
        second = half_inverse(lower + shift - dot(w, cross, ((1,), (1,))), rows_ref.at[1])
        x = dot(second, w)
        store_packed(out_ref, first + dot(w, x, ((0,), (0,))), -x, second)


def unpack_kernel(here_ref, *refs):
    in_refs, (full_ref, mine_ref, theirs_ref, block_ref, done) = refs[:N_Z], refs[N_Z:]
    c, own = here_ref[2], own_slot(here_ref)
    start = (here_ref[0] * N_Z + here_ref[1]) * 2

    def rows(k, core):
        return block_ref[k, pl.ds(pl.multiple_of((start + core) * SUB, SUB), SUB), :]

    def leave(k):
        return pltpu.make_async_copy(block_ref.at[k], full_ref.at[k], done.at[k])

    for offset, ref in zip(OFFSETS, in_refs):
        slot = (own + N_Z + offset) % N_Z
        k = rank(slot, c)

        @pl.when(holds(slot, c))
        def _():
            upper, cross, lower = unpacked(ref[...])
            block_ref[k, 0:HALF, 0:HALF] = upper
            block_ref[k, 0:HALF, HALF:BLK] = cross.T
            block_ref[k, HALF:BLK, 0:HALF] = cross
            block_ref[k, HALF:BLK, HALF:BLK] = lower
            leave(k).start()
            mine_ref[k] = rows(k, c)
            theirs_ref[k] = rows(k, 1 - c)

    for k in range(PER_CORE):
        leave(k).wait()


def precond_kernel(here_ref, owner_ref, own_ref, other_ref, grad_ref, out_ref, table_ref):
    step = pl.program_id(0)
    k = step % PER_CORE

    @pl.when(step < PER_CORE)
    def _():
        out_ref[...] = dot(own_ref[k], grad_ref[...])

    @pl.when(step >= PER_CORE)
    def _():
        out_ref[...] = dot(other_ref[k], grad_ref[...])

    @pl.when(step == 0)
    def _():
        sections, nblocks = owner_ref.shape
        for j in range(HOST):
            table_ref[j] = -1

        def section(s, count):
            for b in range(nblocks):
                hit = owner_ref[s, b] == here_ref[3]

                @pl.when(hit)
                def _(count=count):
                    table_ref[count] = s * nblocks + (b + here_ref[2] * PER_CORE) % nblocks

                count = count + hit.astype(jnp.int32)
            return count

        lax.fori_loop(0, sections, section, jnp.int32(0))


def hosted_kernel(table_ref, rows_ref, out_ref):
    nblocks = rows_ref.shape[1]
    for j in range(HOST):
        source = table_ref[j]
        at = jnp.maximum(source, 0)
        rows = rows_ref[at // nblocks, at % nblocks]
        out_ref[j] = jnp.where(source >= 0, rows, 0.0)


def call(kernel, out_shape, n_smem, n_vmem, scratch=()):
    out_specs = jax.tree.map(lambda _: pl.BlockSpec(memory_space=VMEM), out_shape)
    return pl.pallas_call(
        kernel,
        out_shape=out_shape,
        in_specs=[pl.BlockSpec(memory_space=pltpu.SMEM)] * n_smem
        + [pl.BlockSpec(memory_space=VMEM)] * n_vmem,
        out_specs=out_specs,
        scratch_shapes=scratch,
        compiler_params=pltpu.CompilerParams(vmem_limit_bytes=LIMIT),
    )


def shape(*dims):
    return jax.ShapeDtypeStruct(dims, f32)


IN_VMEM = pl.BlockSpec(memory_space=VMEM)
IN_SMEM = pl.BlockSpec(memory_space=pltpu.SMEM)


def unpack(here, values):
    return pl.pallas_call(
        unpack_kernel,
        out_shape=[shape(PER_CORE, BLK, BLK)] + [shape(PER_CORE, SUB, BLK)] * 2,
        in_specs=[IN_SMEM] + [IN_VMEM] * N_Z,
        out_specs=[pl.BlockSpec(memory_space=pltpu.HBM), IN_VMEM, IN_VMEM],
        scratch_shapes=[VMEM((PER_CORE, BLK, BLK), f32), pltpu.SemaphoreType.DMA((PER_CORE,))],
        compiler_params=pltpu.CompilerParams(vmem_limit_bytes=LIMIT),
    )(here, *values)


def preconditioned(here, owner_of, own, other, grad):
    rows, columns = grad.shape

    def block(i, here_ref):
        c = here_ref[2]
        return jnp.where(i < PER_CORE, c * PER_CORE + i, (1 - c) * PER_CORE + i - PER_CORE), 0

    part = pl.BlockSpec((BLK, columns), block)
    return pl.pallas_call(
        precond_kernel,
        grid_spec=pltpu.PrefetchScalarGridSpec(
            num_scalar_prefetch=1,
            grid=(rows // BLK,),
            in_specs=[IN_SMEM, IN_VMEM, IN_VMEM, part],
            out_specs=[part, IN_SMEM],
        ),
        out_shape=[shape(rows, columns), jax.ShapeDtypeStruct((HOST,), jnp.int32)],
        cost_estimate=pl.CostEstimate(
            flops=12 * rows * BLK * columns, bytes_accessed=16 * rows * columns, transcendentals=0
        ),
        compiler_params=pltpu.CompilerParams(vmem_limit_bytes=LIMIT),
    )(here, owner_of, own, other, grad)


def shards(acts, grad, owner_of):
    section_count = lax.axis_size("pipe")
    all_tokens = acts.shape[1] * lax.axis_size(DP)
    here = jnp.stack([lax.axis_index(a) for a in ("x", "z", "c", "pipe")]).astype(jnp.int32)
    features = acts[0]
    one = shape(TALL, HALF)
    packed = shape(PER_CORE, TALL, HALF)
    got = across_cores(call(functools.partial(gram_kernel, other=True), packed, 1, 1)(here, features))
    mine = call(functools.partial(gram_kernel, other=False), packed, 1, 1)(here, features)
    single = [offset for offset in OFFSETS if offset not in PAIR]
    parts = call(parts_kernel, [shape(2, TALL, HALF)] + [one] * len(single), 1, 2)(here, mine, got)
    part = dict(zip(single, parts[1:]))

    pair = across_x(parts[0])
    far = [along_z(part[2], 2), along_z(part[-2], -2)]
    across = across_x(part[4])
    near = [along_z(part[1] + pair[0], 1), along_z(part[-1] + pair[1], -1)]
    half = part[0] + across + far[0] + far[1] + near[0] + near[1]
    other_half = to_twin(half)
    invert = functools.partial(invert_kernel, all_tokens=all_tokens)
    inverse = call(invert, one, 1, 2, [VMEM((2, HALF, HALF), f32)])(here, half, other_half)

    held = {0: inverse, -1: along_z(inverse, 1), 1: along_z(inverse, -1)}
    held[4] = across_x(inverse)
    held[-2], held[2] = along_z(inverse, 2), along_z(inverse, -2)
    held[3], held[5] = across_x(held[-1]), across_x(held[1])
    own, own_rows, their_rows = unpack(here, [held[k] for k in OFFSETS])
    other_rows = across_cores(their_rows)
    rows = jnp.concatenate([own_rows, other_rows])
    sent = jnp.broadcast_to(rows[None], (section_count, *rows.shape))
    own, sent = lax.optimization_barrier((own, sent))
    other = across_cores(own)
    everyone = lax.all_to_all(sent, "pipe", 0, 0, tiled=True)
    precond, table = preconditioned(here, owner_of, own, other, grad)
    hosted = call(hosted_kernel, shape(HOST, SUB, BLK), 1, 1)(table, everyone)
    return (precond, hosted[None])


def solution(mesh):
    torus = Mesh(mesh.devices.reshape(mesh.shape["pipe"], 2, N_Z, 2), ("pipe", "x", "z", "c"))
    placed = (P("pipe", DP, None), P("pipe", DP), P())
    return jax.shard_map(
        shards,
        mesh=torus,
        in_specs=placed,
        out_specs=(P("pipe", DP), P("pipe", None, DP, None)),
        check_vma=False,
    )
```

```python
import functools

import jax
import jax.numpy as jnp
from jax import lax
from jax.experimental import pallas as pl
from jax.experimental.pallas import tpu as pltpu
from jax.sharding import Mesh
from jax.sharding import PartitionSpec as P

BLK = 256
HALF = BLK // 2
SUB = 8
NB = 12
PER_CORE = NB // 2
HOST = 24
TALL = 2 * HALF + SUB
N_Z = 8
DP = ("x", "z", "c")
damping_ratio = 0.1
LIMIT = 8 * 1024 * 1024
VMEM = pltpu.VMEM
f32 = jnp.float32


def own_slot(here_ref):
    return (here_ref[1] + 4 * here_ref[0]) % N_Z


def holds(slot, c):
    return (slot % 4) != jnp.where(c == 0, 3, 1)


def rank(slot, c):
    return (slot // 4) * 3 + jnp.where(c == 0, slot % 4, (slot % 4 + 1) // 2)


OFFSETS = (0, 1, -1, 2, -2, 3, 4, 5)
PAIR = (5, 3)


def along_z(value, step):
    return lax.ppermute(value, "z", [(z, (z + step) % N_Z) for z in range(N_Z)])


def across_x(value):
    return lax.ppermute(value, "x", [(0, 1), (1, 0)])


def to_twin(value):
    pairs = [(x * N_Z + z, (1 - x) * N_Z + (z + 4) % N_Z) for x in range(2) for z in range(N_Z)]
    return lax.ppermute(value, ("x", "z"), pairs)


def across_cores(value):
    return lax.ppermute(value, "c", [(0, 1), (1, 0)])


def grids():
    return (
        lax.broadcasted_iota(jnp.int32, (HALF, HALF), 0),
        lax.broadcasted_iota(jnp.int32, (HALF, HALF), 1),
    )


def store_packed(ref, upper, cross, lower):
    i, j = grids()
    ref[0:HALF, :] = cross
    ref[HALF:BLK, :] = jnp.where(i >= j, upper, lower)
    ref[BLK:TALL, :] = jnp.broadcast_to(
        jnp.sum(jnp.where(i == j, lower, 0.0), axis=0, keepdims=True), (SUB, HALF)
    )


def unpacked(value):
    i, j = grids()
    cross, mixed, diagonal = value[0:HALF], value[HALF:BLK], value[BLK : BLK + 1]
    turned = mixed.T
    upper = jnp.where(i >= j, mixed, turned)
    lower = jnp.where(i < j, mixed, jnp.where(i > j, turned, diagonal))
    return upper, cross, lower


def gram_kernel(here_ref, acts_ref, out_ref, *, other):
    c = here_ref[2]
    first = (1 - c if other else c) * PER_CORE
    for k in range(PER_CORE):
        start = pl.multiple_of((first + k) * BLK, BLK)
        part = acts_ref[:, pl.ds(start, BLK)]
        total = lax.dot_general(part, part, (((0,), (0,)), ((), ())), preferred_element_type=f32)
        store_packed(
            out_ref.at[k], total[0:HALF, 0:HALF], total[HALF:BLK, 0:HALF], total[HALF:BLK, HALF:BLK]
        )


def parts_kernel(here_ref, mine_ref, got_ref, pair_ref, *out_refs):
    c, own = here_ref[2], own_slot(here_ref)
    single = [offset for offset in OFFSETS if offset not in PAIR]
    targets = [(offset, pair_ref.at[n]) for n, offset in enumerate(PAIR)] + list(zip(single, out_refs))
    for offset, out_ref in targets:
        slot = (own + N_Z + offset) % N_Z
        k = rank(slot, c)

        @pl.when(holds(slot, c))
        def _():
            out_ref[...] = mine_ref[k] + got_ref[k]


def small_inverse(d):
    d = dict(d)

    def at(i, j):
        return d[(i, j)] if i >= j else d[(j, i)]

    for k in range(SUB):
        inv = 1.0 / at(k, k)
        b = {i: at(i, k) * inv for i in range(SUB) if i != k}
        for i in b:
            for j in b:
                if j <= i:
                    d[(i, j)] = d[(i, j)] - b[i] * at(j, k)
        for i in b:
            d[(max(i, k), min(i, k))] = b[i]
        d[(k, k)] = -inv
    return d


def summed(terms):
    while len(terms) > 1:
        terms = [terms[n] + terms[n + 1] for n in range(0, len(terms), 2)]
    return terms[0]


def dot(a, b, dims=((1,), (0,))):
    return lax.dot_general(
        a, b, (dims, ((), ())), precision=lax.Precision.HIGHEST, preferred_element_type=f32
    )


def half_factors(value, rows_ref):
    count = HALF // SUB
    tiles = [value[SUB * v : SUB * v + SUB] for v in range(count)]
    lane = lax.broadcasted_iota(jnp.int32, (SUB, HALF), 1)
    line = lax.broadcasted_iota(jnp.int32, (SUB, HALF), 0)
    lower, scaled = [], []

    def spread(v):
        return jnp.broadcast_to(v, (SUB, HALF))

    for t, pivot in enumerate(tiles):
        first = SUB * t
        inside = (lane >= first) & (lane < first + SUB)
        rows_ref[first : first + SUB, :] = pivot
        each = [rows_ref[pl.ds(first + j, SUB, stride=0), :] for j in range(SUB)]
        minus = small_inverse(
            {
                (i, j): spread(each[i][:, first + j : first + j + 1])
                for i in range(SUB)
                for j in range(i + 1)
            }
        )
        rows = [
            jnp.where(lane == first + j, 1.0, jnp.where(inside, 0.0, each[j])) for j in range(SUB)
        ]
        new = [
            summed([minus[(max(i, j), min(i, j))] * rows[j] for j in range(SUB)])
            for i in range(SUB)
        ]
        own = jnp.zeros((SUB, HALF), f32)
        for j in range(SUB):
            own = jnp.where(line == j, -new[j], own)
        scaled.append(jnp.where(lane < first + SUB, own, 0.0))
        lower.append(jnp.where(lane < first, pivot, jnp.where(lane == line + first, 1.0, 0.0)))
        for v in range(t + 1, count):
            update = summed(
                [spread(tiles[v][:, first + j : first + j + 1]) * new[j] for j in range(SUB)]
            )
            tiles[v] = jnp.where(inside, 0.0, tiles[v]) + update
    return jnp.concatenate(lower, axis=0), jnp.concatenate(scaled, axis=0)


def invert_kernel(here_ref, a_ref, b_ref, out_ref, rows_ref, *, all_tokens):
    @pl.when(holds(own_slot(here_ref), here_ref[2]))
    def _():
        upper, cross, lower = unpacked((a_ref[...] + b_ref[...]) * (1.0 / all_tokens))
        i, j = grids()
        same = i == j
        trace = jnp.sum(
            jnp.sum(jnp.where(same, upper + lower, 0.0), axis=0, keepdims=True), axis=1, keepdims=True
        )
        damping = damping_ratio * trace / BLK
        shift = jnp.where(same, damping, 0.0)
        turned = ((0,), (0,))
        first = dot(*half_factors(upper + shift, rows_ref.at[0]), turned)
        w = dot(cross, first)
        below, scaled = half_factors(lower + shift - dot(w, cross, ((1,), (1,))), rows_ref.at[1])
        left, right = dot(below, w), dot(scaled, w)
        store_packed(
            out_ref, first + dot(left, right, turned), -dot(below, right, turned), dot(below, scaled, turned)
        )


def unpack_kernel(here_ref, *refs):
    in_refs, (full_ref, mine_ref, theirs_ref, block_ref, done) = refs[:N_Z], refs[N_Z:]
    c, own = here_ref[2], own_slot(here_ref)
    start = (here_ref[0] * N_Z + here_ref[1]) * 2

    def rows(k, core):
        return block_ref[k, pl.ds(pl.multiple_of((start + core) * SUB, SUB), SUB), :]

    def leave(k):
        return pltpu.make_async_copy(block_ref.at[k], full_ref.at[k], done.at[k])

    for offset, ref in zip(OFFSETS, in_refs):
        slot = (own + N_Z + offset) % N_Z
        k = rank(slot, c)

        @pl.when(holds(slot, c))
        def _():
            upper, cross, lower = unpacked(ref[...])
            block_ref[k, 0:HALF, 0:HALF] = upper
            block_ref[k, 0:HALF, HALF:BLK] = cross.T
            block_ref[k, HALF:BLK, 0:HALF] = cross
            block_ref[k, HALF:BLK, HALF:BLK] = lower
            leave(k).start()
            mine_ref[k] = rows(k, c)
            theirs_ref[k] = rows(k, 1 - c)

    for k in range(PER_CORE):
        leave(k).wait()


def precond_kernel(here_ref, owner_ref, own_ref, other_ref, grad_ref, out_ref, table_ref):
    step = pl.program_id(0)
    k = step % PER_CORE

    @pl.when(step < PER_CORE)
    def _():
        out_ref[...] = dot(own_ref[k], grad_ref[...])

    @pl.when(step >= PER_CORE)
    def _():
        out_ref[...] = dot(other_ref[k], grad_ref[...])

    @pl.when(step == 0)
    def _():
        sections, nblocks = owner_ref.shape
        for j in range(HOST):
            table_ref[j] = -1

        def section(s, count):
            for b in range(nblocks):
                hit = owner_ref[s, b] == here_ref[3]

                @pl.when(hit)
                def _(count=count):
                    table_ref[count] = s * nblocks + (b + here_ref[2] * PER_CORE) % nblocks

                count = count + hit.astype(jnp.int32)
            return count

        lax.fori_loop(0, sections, section, jnp.int32(0))


def hosted_kernel(table_ref, rows_ref, out_ref):
    nblocks = rows_ref.shape[1]
    for j in range(HOST):
        source = table_ref[j]
        at = jnp.maximum(source, 0)
        rows = rows_ref[at // nblocks, at % nblocks]
        out_ref[j] = jnp.where(source >= 0, rows, 0.0)


def call(kernel, out_shape, n_smem, n_vmem, scratch=()):
    out_specs = jax.tree.map(lambda _: pl.BlockSpec(memory_space=VMEM), out_shape)
    return pl.pallas_call(
        kernel,
        out_shape=out_shape,
        in_specs=[pl.BlockSpec(memory_space=pltpu.SMEM)] * n_smem
        + [pl.BlockSpec(memory_space=VMEM)] * n_vmem,
        out_specs=out_specs,
        scratch_shapes=scratch,
        compiler_params=pltpu.CompilerParams(vmem_limit_bytes=LIMIT),
    )


def shape(*dims):
    return jax.ShapeDtypeStruct(dims, f32)


IN_VMEM = pl.BlockSpec(memory_space=VMEM)
IN_SMEM = pl.BlockSpec(memory_space=pltpu.SMEM)


def unpack(here, values):
    return pl.pallas_call(
        unpack_kernel,
        out_shape=[shape(PER_CORE, BLK, BLK)] + [shape(PER_CORE, SUB, BLK)] * 2,
        in_specs=[IN_SMEM] + [IN_VMEM] * N_Z,
        out_specs=[pl.BlockSpec(memory_space=pltpu.HBM), IN_VMEM, IN_VMEM],
        scratch_shapes=[VMEM((PER_CORE, BLK, BLK), f32), pltpu.SemaphoreType.DMA((PER_CORE,))],
        compiler_params=pltpu.CompilerParams(vmem_limit_bytes=LIMIT),
    )(here, *values)


def preconditioned(here, owner_of, own, other, grad):
    rows, columns = grad.shape

    def block(i, here_ref):
        c = here_ref[2]
        return jnp.where(i < PER_CORE, c * PER_CORE + i, (1 - c) * PER_CORE + i - PER_CORE), 0

    part = pl.BlockSpec((BLK, columns), block)
    return pl.pallas_call(
        precond_kernel,
        grid_spec=pltpu.PrefetchScalarGridSpec(
            num_scalar_prefetch=1,
            grid=(rows // BLK,),
            in_specs=[IN_SMEM, IN_VMEM, IN_VMEM, part],
            out_specs=[part, IN_SMEM],
        ),
        out_shape=[shape(rows, columns), jax.ShapeDtypeStruct((HOST,), jnp.int32)],
        cost_estimate=pl.CostEstimate(
            flops=12 * rows * BLK * columns, bytes_accessed=16 * rows * columns, transcendentals=0
        ),
        compiler_params=pltpu.CompilerParams(vmem_limit_bytes=LIMIT),
    )(here, owner_of, own, other, grad)


def shards(acts, grad, owner_of):
    section_count = lax.axis_size("pipe")
    all_tokens = acts.shape[1] * lax.axis_size(DP)
    here = jnp.stack([lax.axis_index(a) for a in ("x", "z", "c", "pipe")]).astype(jnp.int32)
    features = acts[0]
    one = shape(TALL, HALF)
    packed = shape(PER_CORE, TALL, HALF)
    got = across_cores(call(functools.partial(gram_kernel, other=True), packed, 1, 1)(here, features))
    mine = call(functools.partial(gram_kernel, other=False), packed, 1, 1)(here, features)
    single = [offset for offset in OFFSETS if offset not in PAIR]
    parts = call(parts_kernel, [shape(2, TALL, HALF)] + [one] * len(single), 1, 2)(here, mine, got)
    part = dict(zip(single, parts[1:]))

    pair = across_x(parts[0])
    far = [along_z(part[2], 2), along_z(part[-2], -2)]
    across = across_x(part[4])
    near = [along_z(part[1] + pair[0], 1), along_z(part[-1] + pair[1], -1)]
    half = part[0] + across + far[0] + far[1] + near[0] + near[1]
    other_half = to_twin(half)
    invert = functools.partial(invert_kernel, all_tokens=all_tokens)
    inverse = call(invert, one, 1, 2, [VMEM((2, HALF, HALF), f32)])(here, half, other_half)

    held = {0: inverse, -1: along_z(inverse, 1), 1: along_z(inverse, -1)}
    held[4] = across_x(inverse)
    held[-2], held[2] = along_z(inverse, 2), along_z(inverse, -2)
    held[3], held[5] = across_x(held[-1]), across_x(held[1])
    own, own_rows, their_rows = unpack(here, [held[k] for k in OFFSETS])
    other_rows = across_cores(their_rows)
    rows = jnp.concatenate([own_rows, other_rows])
    sent = jnp.broadcast_to(rows[None], (section_count, *rows.shape))
    own, sent = lax.optimization_barrier((own, sent))
    other = across_cores(own)
    everyone = lax.all_to_all(sent, "pipe", 0, 0, tiled=True)
    precond, table = preconditioned(here, owner_of, own, other, grad)
    hosted = call(hosted_kernel, shape(HOST, SUB, BLK), 1, 1)(table, everyone)
    return (precond, hosted[None])


def solution(mesh):
    torus = Mesh(mesh.devices.reshape(mesh.shape["pipe"], 2, N_Z, 2), ("pipe", "x", "z", "c"))
    placed = (P("pipe", DP, None), P("pipe", DP), P())
    return jax.shard_map(
        shards,
        mesh=torus,
        in_specs=placed,
        out_specs=(P("pipe", DP), P("pipe", None, DP, None)),
        check_vma=False,
    )
```
